32 devices in a mesh: expert: 8 (over z, x), tensor: 4 (over y, core).
Axes of the slice: x: 2, y: 2, z: 4, core: 2. Of those that a mesh axis runs over, the one named last changes fastest.
Arguments:
- layer_input: bfloat16 [16384, 768], P(('expert', 'tensor')), may hold values from -6 to 6
- segment_ids: int32 [8, 2048], P('expert', 'tensor'), may hold values from 0 to 2, never falling along the last dimension, each value on 1 to 1536 neighbouring positions
- routes: int32 [16384, 2], P(('expert', 'tensor')), may hold values from 0 to 7, all different within a row
- gate_values: float32 [16384, 2], P(('expert', 'tensor')), may hold values from 0.2 to 1
- attn_gain: float32 [768], replicated, may hold values from 0.5 to 1.5
- qkv_weight: bfloat16 [3, 768, 768], P(None, None, 'tensor'), may hold values from -0.21875 to 0.21875
- position_bias: float32 [12, 32], P('tensor'), may hold values from -4 to 4
- out_weight: bfloat16 [768, 768], P('tensor'), may hold values from -3.5 to 3.5
- moe_gain: float32 [768], replicated, may hold values from 0.5 to 1.5
- up_weight: bfloat16 [8, 768, 3072], P('expert', None, 'tensor'), may hold values from -0.21875 to 0.21875
- down_weight: bfloat16 [8, 3072, 768], P('expert', 'tensor'), may hold values from -0.109375 to 0.109375
- out_grad: bfloat16 [16384, 768], P(('expert', 'tensor')), may hold values from -6 to 6
Outputs:
- layer_output: bfloat16 [16384, 768], P(('expert', 'tensor'))
- input_grad: float32 [16384, 768], P(('expert', 'tensor'))
- attn_gain_grad: float32 [768], replicated
- qkv_grad: float32 [3, 768, 768], P(None, None, 'tensor')
- position_bias_grad: float32 [12, 32], P('tensor')
- out_weight_grad: float32 [768, 768], P('tensor')
- moe_gain_grad: float32 [768], replicated
- up_grad: float32 [8, 768, 3072], P('expert', None, 'tensor')
- down_grad: float32 [8, 3072, 768], P('expert', 'tensor')
The draws below stay inside these ranges and needn't reach their ends.
Inputs may be any that keep to these rules, and one draw needn't show every extreme that they name: `segment_ids`: within each sequence the segment ids never fall. `routes`: the 2 experts of a token differ.
All inputs are finite; a program needn't handle non-finite values.
Results may differ from the reference program's by a relative error of at most 0.018.
Values may be sent and summed in bfloat16 or wider, within the bound.
No kernel may reach another device: no remote copies, remote signals or barrier semaphores. Data moves between devices by JAX's collectives and lax.ppermute only.
A program may use at most 192 MiB of HBM per device.

```python
import functools
import math
import jax
import jax.numpy as jnp
import numpy as np
from jax import lax

D = 768
HEADS = 12
HEAD = 64
FF = 3072
TOPK = 2
BUCKETS = 32
WINDOW = 1024
QBLOCK = 512
TOK_DEV = 512
SEQ = 2048
SEQS = 8
TOKENS = 16384
EXPERTS = 8
CAP = 160
N_EXPERT = 8
N_TENSOR = 4


def shard_levels(rng, extent, cuts, least, largest):
    factor_of, own = 1.0, jax.random.fold_in(rng, 6)
    for axis_at, parts in cuts:
        heights = jnp.exp(jax.random.uniform(jax.random.fold_in(own, axis_at), (parts,), jnp.float32, least / len(cuts), largest / len(cuts)))
        factor_of = factor_of * jnp.repeat(heights, extent[axis_at] // parts).reshape([-1 if axis == axis_at else 1 for axis in range(len(extent))])
    return factor_of


def distinct(rng, rows, number_of, top, lift):
    order = jax.random.permutation(jax.random.fold_in(rng, 1), number_of)
    favour = order
    for power in range(3):
        favour = favour * favour // number_of
    favour = favour * lift // number_of
    tickets = jax.random.randint(jax.random.fold_in(rng, 2), (rows, number_of), 0, 4096) + favour
    holders = jax.random.permutation(jax.random.fold_in(rng, 3), rows)[jnp.arange(number_of) % rows]
    tickets = jnp.where(jnp.arange(rows)[:, None] == holders[None, :], 1 << 14, tickets)
    priority = tickets * number_of + jnp.arange(number_of)
    return lax.top_k(priority.astype(jnp.int32), top)[1].astype(jnp.int32)


def split_up(amount, total, limit, skew):
    weights = [(1 << 20) // math.isqrt(rank ** skew) + 1 for rank in range(2, amount + 1)]
    rest, given = total - limit - (amount - 1), [1] * (amount - 1)
    while rest > 0:
        free = [i for i in range(amount - 1) if given[i] < limit]
        mass, remaining = sum([weights[i] for i in free]), rest
        for i in free:
            extra = min(limit - given[i], max(1, remaining * weights[i] // mass), rest)
            given[i] = given[i] + extra
            rest = rest - extra
    return np.array([limit] + given)


def uneven_parts(rng, count, total, bound, slope):
    if count == 2:
        one = jax.random.randint(rng, (), max(1, total - bound), min(bound, total - 1) + 1)
        return jnp.stack([one, total - one])
    sizes = jnp.asarray(split_up(count, total, bound, slope), jnp.int32)
    twos = (count - 1) // 2
    donor, sink = sizes[1:1 + 2 * twos:2], sizes[2:2 + 2 * twos:2]
    slack = jnp.minimum(donor - 1, bound - sink)
    shifted = jax.random.randint(jax.random.fold_in(rng, 1), (twos,), 0, 1 << 20) % (slack + 1)
    sizes = sizes.at[1:1 + 2 * twos:2].set(donor - shifted).at[2:2 + 2 * twos:2].set(sink + shifted)
    return sizes[jax.random.permutation(jax.random.fold_in(rng, 2), count)]


def gaussian(key, shape, scale, limit, cuts=(), kind=jnp.bfloat16):
    values = jax.random.normal(key, shape, jnp.float32) * scale
    if len(cuts) > 0:
        values = shard_levels(key, shape, cuts, -0.22, 0.18) * values
    return jnp.clip(values, min=-limit, max=limit).astype(kind)


def setup_inputs(seed: int = 0) -> dict:
    seeds = jax.random.split(jax.random.key(seed), 13)
    layer_input = gaussian(seeds[0], (TOKENS, D), 1.0, 6.0, ((0, 32),))
    segment_ids = jax.vmap(lambda own: jnp.searchsorted(jnp.cumsum(uneven_parts(own, 3, SEQ, SEQ * 3 // 4, 0)), jnp.arange(SEQ), side="right"))(jax.random.split(seeds[1], SEQS)).reshape((SEQS, SEQ)).astype(jnp.int32)
    routes = distinct(seeds[2], TOKENS, EXPERTS, TOPK, 2048)
    gate_values = jnp.clip(0.2 + 0.8 * jax.random.uniform(seeds[3], (TOKENS, TOPK), jnp.float32) ** shard_levels(seeds[3], (TOKENS, TOPK), ((0, 32),), -0.2, 0.2), 0.2, 1.0)
    attn_gain = jnp.clip(1.0 + 0.1 * jax.random.normal(seeds[4], (D,), jnp.float32), 0.5, 1.5)
    qkv_weight = gaussian(seeds[5], (3, D, HEADS * HEAD), D ** -0.5, 0.21875, ((2, 4),))
    position_bias = gaussian(seeds[6], (HEADS, BUCKETS), 1.0, 4.0, ((0, 4),), jnp.float32)
    out_weight = gaussian(seeds[7], (HEADS * HEAD, D), (max(1, HEADS * HEAD // 256)) ** -0.5, 3.5, ((0, 4),))
    moe_gain = jnp.clip(1.0 + 0.1 * jax.random.normal(seeds[8], (D,), jnp.float32), 0.5, 1.5)
    up_weight = gaussian(seeds[9], (EXPERTS, D, FF), D ** -0.5, 0.21875, ((0, 8), (2, 4)))
    down_weight = gaussian(seeds[10], (EXPERTS, FF, D), FF ** -0.5, 0.109375, ((0, 8), (1, 4)))
    out_grad = gaussian(seeds[11], (TOKENS, D), 1.0, 6.0, ((0, 32),))
    return {"layer_input": layer_input, "segment_ids": segment_ids, "routes": routes, "gate_values": gate_values, "attn_gain": attn_gain, "qkv_weight": qkv_weight, "position_bias": position_bias, "out_weight": out_weight, "moe_gain": moe_gain, "up_weight": up_weight, "down_weight": down_weight, "out_grad": out_grad}


@jax.custom_vjp
def low(v):
    return lax.optimization_barrier(v.astype(jnp.bfloat16)).astype(jnp.float32)

@jax.custom_vjp
def low_back(v):
    return v

def low_keep(v):
    return (low(v), None)

def low_pass(kept, grad):
    return (grad,)

def back_keep(v):
    return (v, None)

def back_low(kept, grad):
    return (low(grad),)
low.defvjp(low_keep, low_pass)
low_back.defvjp(back_keep, back_low)
highest = lax.Precision.HIGHEST

def low_both(value):
    return low(low_back(value))

def bucket_edges(buckets):
    half_count = buckets // 2
    edges = list(range(1, half_count))
    for power in range(half_count):
        edges.append(int(math.ceil(half_count * (128.0 / half_count) ** (power / half_count))))
    return edges

def bucket_index(distance, buckets):
    counted = jnp.zeros(distance.shape, jnp.int32)
    for edge in bucket_edges(buckets):
        counted = counted + (distance >= edge).astype(jnp.int32)
    return counted

def norm_rows(values, gain):
    return values * lax.rsqrt(lax.optimization_barrier(jnp.mean(values * values, -1, keepdims=True)) + 1e-06) * gain

def slot_tables(routes, gate_values, experts, capacity):
    rows_here = routes.shape[0]
    pairs = routes.reshape(-1)
    hits = (pairs[:, None] == jnp.arange(experts, dtype=jnp.int32)[None, :]).astype(jnp.int32)
    places = lax.optimization_barrier(jnp.sum((jnp.cumsum(hits, 0) - 1) * hits, 1))
    kept = places < capacity
    slots = jnp.where(kept, pairs * capacity + places, experts * capacity).astype(jnp.int32)
    owners = jnp.arange(pairs.shape[0], dtype=jnp.int32) // routes.shape[1]
    table = jnp.full((experts * capacity + 1,), rows_here, jnp.int32).at[slots].set(owners)[:-1]
    weights = gate_values.reshape(-1) * kept.astype(gate_values.dtype)
    slot_gate = jnp.zeros((experts * capacity + 1,), gate_values.dtype).at[slots].set(weights)[:-1]
    return (slots, weights, table, slot_gate)

def attend_sequence(query, keys, values, segment, table):
    seq_len, heads_here, head_size = query.shape
    span = WINDOW + QBLOCK
    pad_rows = jnp.zeros((WINDOW, heads_here, head_size), query.dtype)
    keys_pad = jnp.concatenate([pad_rows, keys], 0)
    values_pad = jnp.concatenate([pad_rows, values], 0)
    segment_pad = jnp.concatenate([jnp.full((WINDOW,), -1, jnp.int32), segment.astype(jnp.int32)], 0)
    distance = jnp.arange(QBLOCK, dtype=jnp.int32)[:, None] + WINDOW - jnp.arange(span, dtype=jnp.int32)[None, :]
    in_window = (distance >= 0) & (distance < WINDOW)
    bias = jnp.take(table, bucket_index(distance, table.shape[1]), axis=1)
    scale = HEAD ** (-0.5)

    def one_block(block_index):
        first_row = block_index * QBLOCK
        query_block = lax.dynamic_slice_in_dim(query, first_row, QBLOCK, 0)
        key_block = lax.dynamic_slice_in_dim(keys_pad, first_row, span, 0)
        value_block = lax.dynamic_slice_in_dim(values_pad, first_row, span, 0)
        seg_query = lax.dynamic_slice_in_dim(segment.astype(jnp.int32), first_row, QBLOCK, 0)
        seg_key = lax.dynamic_slice_in_dim(segment_pad, first_row, span, 0)
        raw = low_back(jnp.einsum('qhd,khd->hqk', query_block, key_block, precision=highest) * scale)
        allowed = in_window & (seg_query[:, None] == seg_key[None, :])
        score = jnp.where(allowed[None], raw + bias, -1e+30)
        row_max = lax.optimization_barrier(jnp.max(score, -1, keepdims=True))
        exp_terms = jnp.exp(score - row_max)
        prob = exp_terms / lax.optimization_barrier(jnp.sum(exp_terms, -1, keepdims=True))
        return jnp.einsum('hqk,khd->qhd', low(prob), value_block, precision=highest)
    mixed = lax.map(jax.checkpoint(one_block), jnp.arange(seq_len // QBLOCK, dtype=jnp.int32))
    return mixed.reshape(seq_len, heads_here, head_size)

def attend_items(table, item):
    return attend_sequence(item[0], item[1], item[2], item[3], table)

def reference(layer_input, segment_ids, routes, gate_values, attn_gain, qkv_weight, position_bias, out_weight, moe_gain, up_weight, down_weight, out_grad):
    sources = N_EXPERT * N_TENSOR
    slots, weights, table, slot_gate = jax.vmap(lambda rr, gg: slot_tables(rr, gg, EXPERTS, CAP))(routes.reshape(sources, TOK_DEV, TOPK), gate_values.astype(jnp.float32).reshape(sources, TOK_DEV, TOPK))
    offsets = jnp.arange(sources, dtype=jnp.int32)[:, None]
    token_rows = jnp.where(table == TOK_DEV, TOKENS, table + offsets * TOK_DEV).astype(jnp.int32).reshape(-1)
    pair_slots = jnp.where(slots == EXPERTS * CAP, sources * EXPERTS * CAP, slots + offsets * (EXPERTS * CAP)).astype(jnp.int32).reshape(-1)
    pair_weights = weights.reshape(-1)
    segments = segment_ids.astype(jnp.int32)
    width_part = HEADS * HEAD // N_TENSOR
    heads_part = HEADS // N_TENSOR
    hidden_part = FF // N_TENSOR

    def forward_layer(inputs, gain_one, qkv, bias_table, out_w, gain_two, up_w, down_w):
        norm_one = low(norm_rows(inputs, gain_one))
        attn = jnp.zeros(inputs.shape, inputs.dtype)
        for part_index in range(N_TENSOR):
            columns = slice(part_index * width_part, (part_index + 1) * width_part)
            proj = low_both(jnp.einsum('sd,cdh->csh', low_back(norm_one), qkv[:, :, columns], precision=highest))
            proj = proj.reshape(3, SEQS, SEQ, heads_part, HEAD)
            table_part = bias_table[part_index * heads_part:(part_index + 1) * heads_part]
            mixed = lax.map(functools.partial(attend_items, table_part), (proj[0], proj[1], proj[2], segments))
            mixed = low_both(mixed.reshape(TOKENS, width_part))
            attn = attn + low(jnp.dot(mixed, out_w[columns], precision=highest))
        hidden = inputs + low_back(attn)
        norm_two = low(norm_rows(hidden, gain_two))
        padded = jnp.concatenate([norm_two, jnp.zeros((1, D), norm_two.dtype)], 0)
        sent = low_back(padded[token_rows])
        grouped = sent.reshape(sources, EXPERTS, CAP, D).transpose(1, 0, 2, 3).reshape(EXPERTS, sources * CAP, D)

        def one_expert(item):
            rows_here, up_here, down_here = item
            summed = jnp.zeros(rows_here.shape, rows_here.dtype)
            for part_index in range(N_TENSOR):
                units = slice(part_index * hidden_part, (part_index + 1) * hidden_part)
                copied = low_back(rows_here)
                pre = low_back(jnp.dot(copied, up_here[:, units], precision=highest))
                act = low(jax.nn.gelu(pre))
                summed = summed + low(jnp.dot(act, down_here[units], precision=highest))
            return low_both(summed)
        returned = lax.map(jax.checkpoint(one_expert), (grouped, up_w, down_w))
        returned = returned.reshape(EXPERTS, sources, CAP, D).transpose(1, 0, 2, 3).reshape(sources * EXPERTS * CAP, D)
        returned = jnp.concatenate([returned, jnp.zeros((1, D), returned.dtype)], 0)
        picked = returned[pair_slots] * pair_weights[:, None]
        mixture = lax.optimization_barrier(jnp.sum(picked.reshape(TOKENS, TOPK, D), 1))
        return hidden + mixture
    layer_output, pull = jax.vjp(forward_layer, layer_input.astype(jnp.float32), attn_gain.astype(jnp.float32), qkv_weight.astype(jnp.float32), position_bias.astype(jnp.float32), out_weight.astype(jnp.float32), moe_gain.astype(jnp.float32), up_weight.astype(jnp.float32), down_weight.astype(jnp.float32))
    grads = pull(out_grad.astype(jnp.float32))
    return (layer_output.astype(jnp.bfloat16), grads[0], grads[1], grads[2], grads[3], grads[4], grads[5], grads[6], grads[7])
```

```python
import functools
import math

import jax
import jax.numpy as jnp
from jax import lax
from jax.experimental import pallas as pl
from jax.experimental.pallas import tpu as pltpu
from jax.sharding import PartitionSpec as P


WINDOW = 1024
TILE = 256
NEG = -1e30
EPS = 1e-06
BF = jnp.bfloat16
F32 = jnp.float32

EX, TE = "expert", "tensor"
DIAG, PREV, MASK, PLAIN = range(4)


def bucket_edges(buckets):
    half_count = buckets // 2
    edges = list(range(1, half_count))
    for power in range(half_count):
        edges.append(int(math.ceil(half_count * (128.0 / half_count) ** (power / half_count))))
    return edges


def bucket_index(distance, buckets):
    counted = jnp.zeros(distance.shape, jnp.int32)
    for edge in bucket_edges(buckets):
        counted = counted + (distance >= edge).astype(jnp.int32)
    return counted


def dot(left, right, left_dim=1, right_dim=0):
    return lax.dot_general(
        left, right, (((left_dim,), (right_dim,)), ((), ())), preferred_element_type=F32
    )


def swap(value, axis, bit):
    size = lax.axis_size(axis)
    return lax.ppermute(value, axis, [(i, i ^ bit) for i in range(size)])


def vmem(count):
    return [pl.BlockSpec(memory_space=pltpu.VMEM)] * count


def params(mib=56):
    return pltpu.CompilerParams(vmem_limit_bytes=mib << 20)


def anywhere(count):
    return [pl.BlockSpec(memory_space=pl.ANY)] * count


def shape(dims, dtype):
    return jax.ShapeDtypeStruct(dims, dtype)


def proj_kernel(scale, xa_ref, xb_ref, gain, wt_ref, *refs):
    norm, k_ref, qt, vt = refs[-4:]
    x = jnp.where(pl.program_id(0) < 2, xa_ref[...], xb_ref[...]).astype(F32)
    r = lax.rsqrt(jnp.mean(x * x, -1, keepdims=True) + EPS)
    n = (x * r * gain[...]).astype(BF)
    norm[0] = n
    k_ref[0] = dot(n, wt_ref[1], 1, 1).astype(BF)
    qt[0] = (dot(wt_ref[0], n, 1, 1) * scale).astype(BF)
    vt[0] = dot(wt_ref[2], n, 1, 1).astype(BF)


def pair_specs(width):
    return [
        pl.BlockSpec((TILE, width), lambda n: (jnp.minimum(n, 1), 0)),
        pl.BlockSpec((TILE, width), lambda n: (jnp.maximum(n - 2, 0), 0)),
    ]


def project(base, pair, gain, wt, scale, kept):
    width = pair[0].shape[1]
    loc = wt.shape[1]
    dims = ((TILE, width), (TILE, loc), (loc, TILE), (loc, TILE))
    return pl.pallas_call(
        functools.partial(proj_kernel, scale),
        grid=(4,),
        out_shape=[shape((8,) + d, BF) for d in dims],
        in_specs=pair_specs(width)
        + [
            pl.BlockSpec((1, width), lambda n: (0, 0)),
            pl.BlockSpec((3, loc, width), lambda n: (0, 0, 0)),
        ]
        + anywhere(len(kept)),
        out_specs=[pl.BlockSpec((1,) + d, lambda n: (base + n, 0, 0)) for d in dims],
        input_output_aliases={4 + n: n for n in range(len(kept))},
        compiler_params=params(),
    )(*pair, gain, wt, *kept)


def again_kernel(scale, n_ref, wt_ref, q_ref, v_ref, kt_ref):
    n = n_ref[0]
    q_ref[0] = (dot(n, wt_ref[0], 1, 1) * scale).astype(BF)
    v_ref[0] = dot(n, wt_ref[2], 1, 1).astype(BF)
    kt_ref[0] = dot(wt_ref[1], n, 1, 1).astype(BF)


def project_again(norm, wt, scale):
    tiles, _, width = norm.shape
    loc = wt.shape[1]
    nat = pl.BlockSpec((1, TILE, loc), lambda n: (n, 0, 0))
    return pl.pallas_call(
        functools.partial(again_kernel, scale),
        grid=(tiles,),
        out_shape=[shape((tiles, TILE, loc), BF)] * 2 + [shape((tiles, loc, TILE), BF)],
        in_specs=[
            pl.BlockSpec((1, TILE, width), lambda n: (n, 0, 0)),
            pl.BlockSpec((3, loc, width), lambda n: (0, 0, 0)),
        ],
        out_specs=[nat, nat, pl.BlockSpec((1, loc, TILE), lambda n: (n, 0, 0))],
        compiler_params=params(),
    )(norm, wt)


def head_rows(head, size, dims, axis):
    index = lax.broadcasted_iota(jnp.int32, dims, axis)
    return (index >= head * size) & (index < (head + 1) * size)


def first_key(q, c1, c2):
    start = jnp.where(q >= c2, c2, jnp.where(q >= c1, c1, 0))
    return jnp.maximum(start, q - (WINDOW - 1))


def build_bias(line_ref, bias_ref, heads):
    for h in range(heads):
        row = jnp.broadcast_to(line_ref[h : h + 1, :], (TILE, TILE))
        bias_ref[h] = pltpu.roll(row, 0, 1, stride=1, stride_axis=0)


def key_loop(i, c1, c2, tiles):
    start = first_key(i * TILE, c1, c2) // TILE
    full = (first_key(i * TILE + TILE - 1, c1, c2) + TILE - 1) // TILE
    carry = tiles([(i, DIAG), (i - 1, PREV)], None)
    count = jnp.maximum(i - 1 - start, 0)
    plain = jnp.minimum(jnp.maximum(i - 1 - full, 0), count)
    carry = lax.fori_loop(0, plain, lambda n, c: tiles([(i - 2 - n, PLAIN)], c), carry)
    return lax.fori_loop(plain, count, lambda n, c: tiles([(i - 2 - n, MASK)], c), carry)


def tile_masks(tiles, low, t):
    kk = lax.broadcasted_iota(jnp.int32, (TILE, TILE), 0)
    qq = lax.broadcasted_iota(jnp.int32, (TILE, TILE), 1)
    out = []
    for j, kind in tiles:
        ok = None
        if kind != PLAIN:
            ok = kk >= low - j * TILE
            if kind == DIAG:
                ok = ok & (kk <= qq)
        out.append((jnp.maximum(j, 0) ^ (2 * t), kind, ok))
    return out, qq < kk


def add_bias(s, kind, bias, wrapped):
    if kind == DIAG:
        return s + bias
    if kind == PREV:
        return s + jnp.where(wrapped, bias, 0.0)
    return s


def attn_fwd_kernel(heads, size, base, s_ref, c_ref, k_ref, qt_ref, vt_ref, line_ref, wo_ref, *refs):
    mix_ref, lse_ref, pa_ref, pb_ref, bias_ref = refs[-5:]
    t, c1, c2 = s_ref[0], c_ref[0, 0], c_ref[0, 1]
    loc = heads * size
    step = pl.program_id(0)

    @pl.when(step == 0)
    def _():
        build_bias(line_ref, bias_ref, heads)

    i = (base + step) ^ (2 * t)
    qt = qt_ref[0]
    zero = jnp.zeros_like(qt)
    qz = [jnp.where(head_rows(h, size, (loc, TILE), 0), qt, zero) for h in range(heads)]
    qpos = i * TILE + lax.broadcasted_iota(jnp.int32, (1, TILE), 1)
    low = first_key(qpos, c1, c2)

    def tiles(pairs, carry):
        pairs, wrapped = tile_masks(pairs, low, t)
        scores = []
        for h in range(heads):
            for at, kind, ok in pairs:
                s = add_bias(dot(k_ref[at], qz[h]), kind, bias_ref[h], wrapped)
                scores.append(s if ok is None else jnp.where(ok, s, NEG))
        out = []
        for h in range(heads):
            mine = scores[h * len(pairs) : (h + 1) * len(pairs)]
            m = functools.reduce(jnp.maximum, mine)
            m = jnp.max(m, 0, keepdims=True)
            if carry is not None:
                m = jnp.maximum(carry[h][0], m)
            probs = [jnp.exp(s - m) for s in mine]
            total = jnp.sum(functools.reduce(jnp.add, probs), 0, keepdims=True)
            acc = None
            for (at, _, _), p in zip(pairs, probs):
                piece = dot(vt_ref[at][h * size : (h + 1) * size], p.astype(BF))
                acc = piece if acc is None else acc + piece
            if carry is not None:
                decay = jnp.exp(carry[h][0] - m)
                total = decay * carry[h][1] + total
                acc = decay * carry[h][2] + acc
            out.append((m, total, acc))
        return tuple(out)

    final = key_loop(i, c1, c2, tiles)
    mixed = []
    for h in range(heads):
        m, total, acc = final[h]
        mixed.append((acc * (1.0 / total)).astype(BF))
        lse_ref[0, h : h + 1, :] = m + jnp.log(total)
    mixed = jnp.concatenate(mixed, 0)
    mix_ref[0] = mixed
    part = dot(mixed, wo_ref[...], 0, 0).astype(BF)

    @pl.when(step < 2)
    def _():
        pa_ref[...] = part

    @pl.when(step >= 2)
    def _():
        pb_ref[...] = part


def attn_fwd(base, scal, counts, k, qt, vt, line, wo, kept, heads, size):
    tiles, _, loc = k.shape
    width = wo.shape[1]
    tile = lambda n: (base + n, 0, 0)
    return pl.pallas_call(
        functools.partial(attn_fwd_kernel, heads, size, base),
        grid=(4,),
        out_shape=(
            shape((tiles, loc, TILE), BF),
            shape((tiles, 8, TILE), F32),
            shape((2 * TILE, width), BF),
            shape((2 * TILE, width), BF),
        ),
        in_specs=[
            pl.BlockSpec(memory_space=pltpu.SMEM),
            pl.BlockSpec(memory_space=pltpu.SMEM),
            pl.BlockSpec((tiles, TILE, loc), lambda n: (0, 0, 0)),
            pl.BlockSpec((1, loc, TILE), tile),
            pl.BlockSpec((tiles, loc, TILE), lambda n: (0, 0, 0)),
            pl.BlockSpec((8, TILE), lambda n: (0, 0)),
            pl.BlockSpec((loc, width), lambda n: (0, 0)),
        ]
        + anywhere(len(kept)),
        out_specs=(
            pl.BlockSpec((1, loc, TILE), tile),
            pl.BlockSpec((1, 8, TILE), tile),
            *pair_specs(width),
        ),
        scratch_shapes=[pltpu.VMEM((heads, TILE, TILE), F32)],
        input_output_aliases={7 + n: n for n in range(len(kept))},
        compiler_params=params(),
    )(scal, counts, k, qt, vt, line, wo, *kept)


def attn_bwd_kernel(
    heads,
    size,
    base,
    last,
    s_ref,
    c_ref,
    k_ref,
    v_ref,
    kt_ref,
    qt_ref,
    q_ref,
    da_ref,
    db_ref,
    mix_ref,
    lse_ref,
    line_ref,
    wo_ref,
    *refs,
):
    bias_ref = refs[-1]
    if last:
        dk_in, dv_in, g_in, _, dq_ref, dk_out, dv_out, gl_ref, dk_ref, dv_ref, g_ref = refs[:-1]
    else:
        dq_ref, dk_ref, dv_ref, g_ref = refs[:-1]
    t, c1, c2 = s_ref[0], c_ref[0, 0], c_ref[0, 1]
    loc = heads * size
    step = pl.program_id(0)

    @pl.when(step == 0)
    def _():
        build_bias(line_ref, bias_ref, heads)
        if last:
            dk_ref[...] = dk_in[...]
            dv_ref[...] = dv_in[...]
            g_ref[...] = g_in[...]
        else:
            dk_ref[...] = jnp.zeros_like(dk_ref)
            dv_ref[...] = jnp.zeros_like(dv_ref)
            g_ref[...] = jnp.zeros_like(g_ref)

    i = (base + step) ^ (2 * t)
    rows = jnp.where(step < 2, da_ref[...], db_ref[...])
    dn = dot(rows, wo_ref[...], 1, 1).astype(BF)
    dt = dot(wo_ref[...], rows, 1, 1).astype(BF)
    qt = qt_ref[0]
    qn = q_ref[0]
    zt = jnp.zeros_like(qt)
    zn = jnp.zeros_like(qn)
    rh = [head_rows(h, size, (loc, TILE), 0) for h in range(heads)]
    ch = [head_rows(h, size, (TILE, loc), 1) for h in range(heads)]
    qz = [jnp.where(rh[h], qt, zt) for h in range(heads)]
    dz = [jnp.where(rh[h], dt, zt) for h in range(heads)]
    qm = [jnp.where(ch[h], qn, zn) for h in range(heads)]
    dm = [jnp.where(ch[h], dn, zn) for h in range(heads)]
    prod = dt.astype(F32) * mix_ref[0].astype(F32)
    delta = [jnp.sum(prod[h * size : (h + 1) * size], 0, keepdims=True) for h in range(heads)]
    lse = [lse_ref[0, h : h + 1, :] for h in range(heads)]
    qpos = i * TILE + lax.broadcasted_iota(jnp.int32, (1, TILE), 1)
    low = first_key(qpos, c1, c2)

    def tiles(pairs, carry):
        pairs, wrapped = tile_masks(pairs, low, t)
        out = [None] * heads if carry is None else list(carry)
        raw = [[(dot(k_ref[at], qz[h]), dot(v_ref[at], dz[h])) for h in range(heads)] for at, _, _ in pairs]
        narrow = []
        for (at, kind, ok), products in zip(pairs, raw):
            lows = []
            for h, (s, dp) in enumerate(products):
                s = add_bias(s, kind, bias_ref[h], wrapped) - lse[h]
                if ok is not None:
                    s = jnp.where(ok, s, NEG)
                p = jnp.exp(s)
                ds = p * (dp - delta[h])
                if kind == DIAG:
                    g_ref[h] += ds
                elif kind == PREV:
                    g_ref[h] += jnp.where(wrapped, ds, 0.0)
                lows.append((p.astype(BF), ds.astype(BF)))
            narrow.append(lows)
        for (at, _, _), lows in zip(pairs, narrow):
            dv = None
            dk = None
            for h, (p, ds) in enumerate(lows):
                piece = dot(p, dm[h])
                dv = piece if dv is None else dv + piece
                piece = dot(ds, qm[h])
                dk = piece if dk is None else dk + piece
                piece = dot(kt_ref[at][h * size : (h + 1) * size], ds)
                out[h] = piece if out[h] is None else out[h] + piece
            dv_ref[at] += dv
            dk_ref[at] += dk
        return tuple(out)

    final = key_loop(i, c1, c2, tiles)
    dq_ref[...] = (jnp.concatenate(final, 0) * (size**-0.5)).astype(BF)

    if last:

        @pl.when(step == pl.num_programs(0) - 1)
        def _():
            dk_out[...] = dk_ref[...].astype(BF)
            dv_out[...] = dv_ref[...].astype(BF)
            kk = lax.broadcasted_iota(jnp.int32, (TILE, TILE), 0)
            qq = lax.broadcasted_iota(jnp.int32, (TILE, TILE), 1)
            flip = (kk + qq == TILE - 1).astype(F32)
            for h in range(heads):
                g = lax.dot_general(
                    flip,
                    g_ref[h],
                    (((1,), (0,)), ((), ())),
                    precision=lax.Precision.HIGHEST,
                    preferred_element_type=F32,
                )
                g = pltpu.roll(g, 0, 1, stride=1, stride_axis=0)
                gl_ref[h : h + 1, :] = jnp.sum(g, 0, keepdims=True)


def attn_bwd(base, scal, counts, k, v, kt, qt, q, d_rows, mix, lse, line, wo, sums, heads, size):
    tiles, _, loc = k.shape
    width = wo.shape[1]
    last = bool(sums)
    tile = lambda n: (base + n, 0, 0)
    whole = lambda *dims: pl.BlockSpec(dims, lambda n: (0,) * len(dims))
    nat = whole(tiles, TILE, loc)
    square = whole(heads, TILE, TILE)
    sums_f32 = [shape((tiles, TILE, loc), F32)] * 2 + [shape((heads, TILE, TILE), F32)]
    dq_shape = shape((loc, tiles * TILE), BF)
    dq_spec = pl.BlockSpec((loc, TILE), lambda n: (0, base + n))
    in_specs = [
        pl.BlockSpec(memory_space=pltpu.SMEM),
        pl.BlockSpec(memory_space=pltpu.SMEM),
        nat,
        nat,
        whole(tiles, loc, TILE),
        pl.BlockSpec((1, loc, TILE), tile),
        pl.BlockSpec((1, TILE, loc), tile),
        pl.BlockSpec((TILE, width), lambda n: (jnp.minimum(n, 1), 0)),
        pl.BlockSpec((TILE, width), lambda n: (jnp.maximum(n - 2, 0), 0)),
        pl.BlockSpec((1, loc, TILE), tile),
        pl.BlockSpec((1, 8, TILE), tile),
        whole(8, TILE),
        whole(loc, width),
    ]
    if last:
        in_specs += [nat, nat, square] + anywhere(1)
        out_shape = [dq_shape] + [shape((tiles, TILE, loc), BF)] * 2 + [shape((8, TILE), F32)]
        out_specs = [dq_spec, nat, nat, whole(8, TILE)]
        scratch = [pltpu.VMEM((tiles, TILE, loc), F32)] * 2 + [pltpu.VMEM((heads, TILE, TILE), F32)]
        aliases = {16: 0}
    else:
        out_shape = [dq_shape] + sums_f32
        out_specs = [dq_spec, nat, nat, square]
        scratch = []
        aliases = {}
    return pl.pallas_call(
        functools.partial(attn_bwd_kernel, heads, size, base, last),
        grid=(4,),
        out_shape=out_shape,
        in_specs=in_specs,
        out_specs=out_specs,
        scratch_shapes=scratch + [pltpu.VMEM((heads, TILE, TILE), F32)],
        input_output_aliases=aliases,
        compiler_params=params(),
    )(scal, counts, k, v, kt, qt, q, *d_rows, mix, lse, line, wo, *sums)


def norm_part_kernel(dq_ref, dk_ref, dv_ref, wt_ref, pa_ref, pb_ref):
    step = pl.program_id(0)
    part = dot(dq_ref[...], wt_ref[0], 0, 0) + dot(dk_ref[0], wt_ref[1]) + dot(dv_ref[0], wt_ref[2])

    @pl.when(step < 2)
    def _():
        pa_ref[...] = part.astype(BF)

    @pl.when(step >= 2)
    def _():
        pb_ref[...] = part.astype(BF)


def norm_part(base, dq, dk, dv, wt):
    loc = dq.shape[0]
    width = wt.shape[2]
    tile = lambda n: (base + n, 0, 0)
    return pl.pallas_call(
        norm_part_kernel,
        grid=(4,),
        out_shape=[shape((2 * TILE, width), BF)] * 2,
        in_specs=[
            pl.BlockSpec((loc, TILE), lambda n: (0, base + n)),
            pl.BlockSpec((1, TILE, loc), tile),
            pl.BlockSpec((1, TILE, loc), tile),
            pl.BlockSpec((3, loc, width), lambda n: (0, 0, 0)),
        ],
        out_specs=[
            pl.BlockSpec((TILE, width), lambda n: (jnp.minimum(n, 1), 0)),
            pl.BlockSpec((TILE, width), lambda n: (jnp.maximum(n - 2, 0), 0)),
        ],
        compiler_params=params(),
    )(dq, dk, dv, wt)


def out_grad_kernel(mix_ref, d0, d1, d2, d3, out_ref):
    total = None
    for pos, d_ref in enumerate((d0, d1, d2, d3)):
        for half in range(2):
            piece = dot(mix_ref[2 * pos + half], d_ref[half * TILE : (half + 1) * TILE])
            total = piece if total is None else total + piece
    out_ref[...] = total


def out_grads(mix, d_rows):
    return pl.pallas_call(
        out_grad_kernel,
        out_shape=shape((mix.shape[1], d_rows[0].shape[1]), F32),
        in_specs=vmem(5),
        out_specs=vmem(1)[0],
        compiler_params=params(),
    )(mix, *d_rows)


def proj_grad_kernel(
    chunks, heads, s_ref, dq_ref, dk_ref, dv_ref, norm_ref, wt_ref, og_ref, gl_ref, moe_ref, gain_ref, *refs
):
    outs, (sum_ref, small_ref) = refs[:-2], refs[-2:]
    loc = dq_ref.shape[0]
    n = norm_ref[...]
    total = None
    for c, piece in enumerate((dot(dq_ref[...], n), dot(dk_ref[...], n, 0, 0), dot(dv_ref[...], n, 0, 0))):
        sum_ref[c * loc : (c + 1) * loc] = piece
        line = jnp.sum(piece * wt_ref[c].astype(F32), 0, keepdims=True)
        total = line if total is None else total + line
    sum_ref[3 * loc : 4 * loc] = og_ref[...]
    small_ref[...] = jnp.zeros_like(small_ref)
    small_ref[0:1] = total / gain_ref[...]
    small_ref[1:2] = moe_ref[0:1]
    small_ref[2 : 2 + heads, 0:TILE] = gl_ref[0:heads]
    if chunks == 1:
        outs[0][...] = sum_ref[...]
        outs[1][...] = small_ref[...]
    else:
        rows = 4 * loc // chunks
        small = small_ref[...].astype(BF)
        for e in range(chunks):
            first = pl.multiple_of((s_ref[1] ^ e) * rows, 16)
            outs[e][0:rows] = sum_ref[pl.ds(first, rows)].astype(BF)
            outs[e][rows : rows + 16] = small


def proj_grads(scal, dq, dk, dv, norm, wt, out_part, g_line, moe_part, gain, chunks, heads):
    loc, tokens = dq.shape
    width = wt.shape[2]
    if chunks == 1:
        outs = [((4 * loc, width), F32), ((16, width), F32)]
    else:
        outs = [((4 * loc // chunks + 16, width), BF)] * chunks
    flat = lambda value: value.reshape(tokens, value.shape[-1])
    return pl.pallas_call(
        functools.partial(proj_grad_kernel, chunks, heads),
        out_shape=[shape(dims, kind) for dims, kind in outs],
        in_specs=[pl.BlockSpec(memory_space=pltpu.SMEM)] + vmem(9),
        out_specs=vmem(len(outs)),
        scratch_shapes=[pltpu.VMEM((4 * loc, width), F32), pltpu.VMEM((16, width), F32)],
        compiler_params=params(),
    )(scal, dq, flat(dk), flat(dv), flat(norm), wt, out_part, g_line, moe_part, gain)


def sum_grads_kernel(*refs):
    parts, (out_ref, small_ref) = refs[:-2], refs[-2:]
    total = functools.reduce(jnp.add, [part[...].astype(F32) for part in parts])
    rows = out_ref.shape[0]
    out_ref[...] = total[0:rows].astype(BF)
    small_ref[...] = total[rows:]


def sum_grads(parts):
    rows, width = parts[0].shape
    return pl.pallas_call(
        sum_grads_kernel,
        out_shape=[shape((rows - 16, width), BF), shape((16, width), F32)],
        in_specs=vmem(len(parts)),
        out_specs=vmem(2),
        compiler_params=params(),
    )(*parts)


def unpack_kernel(s_ref, *refs):
    parts, (proj_ref, out_ref) = refs[:-2], refs[-2:]
    rows = parts[0].shape[0]
    edge = proj_ref.shape[0] // rows
    for e, part in enumerate(parts):
        at = s_ref[1] ^ e

        @pl.when(at < edge)
        def _():
            proj_ref[pl.ds(pl.multiple_of(at * rows, 16), rows)] = part[...].astype(F32)

        @pl.when(at >= edge)
        def _():
            out_ref[pl.ds(pl.multiple_of((at - edge) * rows, 16), rows)] = part[...].astype(F32)


def unpack_grads(scal, parts, loc):
    width = parts[0].shape[1]
    return pl.pallas_call(
        unpack_kernel,
        out_shape=[shape((3 * loc, width), F32), shape((loc, width), F32)],
        in_specs=[pl.BlockSpec(memory_space=pltpu.SMEM)] + vmem(len(parts)),
        out_specs=vmem(2),
        compiler_params=params(),
    )(scal, *parts)


def turn_sum_kernel(a_ref, b_ref, c_ref, out_ref):
    out_ref[...] = (a_ref[...].astype(F32) + b_ref[...].astype(F32) + c_ref[...].astype(F32)).T


def turn_sum(a, b, c):
    return pl.pallas_call(
        turn_sum_kernel,
        grid=(3,),
        out_shape=shape(a.shape[::-1], F32),
        in_specs=[pl.BlockSpec((a.shape[0], a.shape[1] // 3), lambda n: (0, n))] * 3,
        out_specs=pl.BlockSpec((a.shape[1] // 3, a.shape[0]), lambda n: (n, 0)),
        compiler_params=params(),
    )(a, b, c)


def select_rows(slot_rows, first, count, ranks):
    want = first + lax.broadcasted_iota(jnp.int32, (count, slot_rows.shape[1]), 0)
    return [(slot_rows[r : r + 1, :] == want).astype(BF) for r in ranks]


def send_grad_kernel(
    experts_all, capacity, groups, direct, s_ref, route_ref, gate_ref, grad_ref, rows_ref, cols_ref, gcol_ref, out_ref
):
    tokens = route_ref.shape[1]
    expert = lax.broadcasted_iota(jnp.int32, (max(8, experts_all), tokens), 0)
    hit = [route_ref[r : r + 1, :] == expert for r in range(2)]
    both = hit[0].astype(BF) + hit[1].astype(BF)
    first = lax.broadcasted_iota(jnp.int32, (tokens, tokens), 0)
    later = lax.broadcasted_iota(jnp.int32, (tokens, tokens), 1)
    earlier = dot(both, (first < later).astype(BF))
    rows = []
    for mask in (0, s_ref[1] if direct else 0):
        for r in range(2):
            place = jnp.sum(jnp.where(hit[r], earlier, 0.0), 0, keepdims=True).astype(jnp.int32)
            slot = (route_ref[r : r + 1, :] ^ mask) * capacity + place
            rows.append(jnp.where(place < capacity, slot, -1))
    rows = jnp.concatenate(rows + rows, 0)
    rows_ref[...] = rows
    cols_ref[...] = rows.astype(F32).T.astype(jnp.int32)
    gates = jnp.concatenate([gate_ref[...]] * 4, 0).T
    gcol_ref[...] = gates
    grad = grad_ref[...].astype(F32)
    scaled = [(grad * gates[:, r : r + 1]).astype(BF) for r in range(2)]
    count = out_ref.shape[0] // groups
    for e in range(groups):
        hot = select_rows(rows_ref, e * count, count, (0, 1))
        out_ref[e * count : (e + 1) * count] = (dot(hot[0], scaled[0]) + dot(hot[1], scaled[1])).astype(BF)


def send_grad(scal, routes, gates, grad, experts_all, capacity, direct):
    tokens, width = grad.shape
    groups = experts_all if direct else 4
    return pl.pallas_call(
        functools.partial(send_grad_kernel, experts_all, capacity, groups, direct),
        out_shape=[
            shape((8, tokens), jnp.int32),
            shape((tokens, 8), jnp.int32),
            shape((tokens, 8), F32),
            shape((experts_all * capacity, width), BF),
        ],
        in_specs=[pl.BlockSpec(memory_space=pltpu.SMEM)] + vmem(3),
        out_specs=vmem(4),
        compiler_params=params(),
    )(scal, routes, gates, grad)


def send_rows_kernel(rows_each, slot_ref, x_ref, p0, r0, r2, gain, hid_ref, *outs):
    attn = p0[...].astype(F32) + r0[...].astype(F32) + r2[...].astype(F32)
    hidden = x_ref[...].astype(F32) + attn
    hid_ref[...] = hidden
    r = lax.rsqrt(jnp.mean(hidden * hidden, -1, keepdims=True) + EPS)
    norm = (hidden * r * gain[...]).astype(BF)
    for e, out in enumerate(outs):
        hot = select_rows(slot_ref, e * rows_each, rows_each, (2, 3))
        out[...] = dot(hot[0] + hot[1], norm).astype(BF)


def send_rows(slot_rows, x, p0, r0, r2, gain, groups, rows_each):
    rows, width = x.shape
    return pl.pallas_call(
        functools.partial(send_rows_kernel, rows_each),
        out_shape=[shape((rows, width), F32)] + [shape((rows_each, width), BF)] * groups,
        in_specs=vmem(6),
        out_specs=vmem(1 + groups),
        compiler_params=params(),
    )(slot_rows, x, p0, r0, r2, gain)


def gather_pairs(slot_cols, blocks, rank_sets, base):
    rows = slot_cols.shape[0]
    sums = [None] * len(rank_sets)
    first = 0
    for block in blocks:
        count = block.shape[0]
        want = first + lax.broadcasted_iota(jnp.int32, (rows, count), 1)
        hot = [(slot_cols[:, base + r : base + r + 1] == want).astype(BF) for r in range(2)]
        data = block[...]
        for n, ranks in enumerate(rank_sets):
            pick = hot[ranks[0]] if len(ranks) == 1 else hot[0] + hot[1]
            piece = dot(pick, data)
            sums[n] = piece if sums[n] is None else sums[n] + piece
        first += count
    return sums


def combine_bwd_kernel(groups, slot_ref, hid_ref, gain, grad_ref, *refs):
    blocks, (dh_ref, da_ref, gg_ref) = refs[:groups], refs[groups:]
    (d,) = gather_pairs(slot_ref, blocks, ((0, 1),), 2)
    hidden = hid_ref[...]
    r = lax.rsqrt(jnp.mean(hidden * hidden, -1, keepdims=True) + EPS)
    u = hidden * r
    gg_ref[...] = jnp.broadcast_to(jnp.sum(u * d, 0, keepdims=True), gg_ref.shape)
    gd = gain[...] * d
    dv = r * (gd - u * jnp.mean(u * gd, -1, keepdims=True))
    d_hidden = grad_ref[...].astype(F32) + dv
    dh_ref[...] = d_hidden
    da_ref[...] = d_hidden.astype(BF)


def combine_bwd(slot_cols, hidden, gain, grad, blocks):
    rows, width = hidden.shape
    groups = len(blocks)
    return pl.pallas_call(
        functools.partial(combine_bwd_kernel, groups),
        out_shape=(shape((rows, width), F32), shape((rows, width), BF), shape((8, width), F32)),
        in_specs=vmem(4 + groups),
        out_specs=vmem(3),
        compiler_params=params(),
    )(slot_cols, hidden, gain, grad, *blocks)


def combine_fwd_kernel(groups, slot_ref, gate_ref, hid_ref, *refs):
    blocks, out_ref = refs[:groups], refs[groups]
    first, second = gather_pairs(slot_ref, blocks, ((0,), (1,)), 0)
    mixture = gate_ref[:, 0:1] * first + gate_ref[:, 1:2] * second
    out_ref[...] = (hid_ref[...] + mixture).astype(BF)


def combine_fwd(slot_cols, gates, hidden, blocks):
    groups = len(blocks)
    return pl.pallas_call(
        functools.partial(combine_fwd_kernel, groups),
        out_shape=shape(hidden.shape, BF),
        in_specs=vmem(3 + groups),
        out_specs=vmem(1)[0],
        compiler_params=params(),
    )(slot_cols, gates, hidden, *blocks)


GELU_C = math.sqrt(2.0 / math.pi)
GELU_A = 0.044715
STRIP = 320


def expert_kernel(groups, rows_each, first_row, members, direct, kept, s_ref, *refs):
    refs = list(refs)
    take = lambda count: [refs.pop(0) for _ in range(count)]
    parts = 4
    ups, downs, xs = take(parts), take(parts), take(groups)
    (d_in_ref,) = take(1)
    take(4 if kept else 0)
    act_out, dpre_out, x_out, d_out = take(4)
    results = take(groups)
    up_ref, down_ref, act_ref, dpre_ref, x_all, d_all, acc_ref, in_sem, d_sem, out_sem, row_sem = refs
    rows = groups * rows_each
    span = pl.ds(first_row, rows)
    own = []
    for n, e in enumerate(members):
        source = (s_ref[1] ^ e) if direct else 0
        own.append(
            pltpu.make_async_copy(
                d_in_ref.at[source], d_all.at[pl.ds(n * rows_each, rows_each)], d_sem.at[n]
            )
        )
        own[n].start()
    for p in range(parts):
        pltpu.make_async_copy(ups[p], up_ref.at[p], in_sem.at[0, p]).start()
        pltpu.make_async_copy(downs[p], down_ref.at[p], in_sem.at[1, p]).start()
    for e in range(groups):
        x_all[e * rows_each : (e + 1) * rows_each] = xs[e][...]
    acc_ref[...] = jnp.zeros_like(acc_ref)
    for copy in own:
        copy.wait()
    joined = [
        pltpu.make_async_copy(x_all, x_out.at[span], row_sem.at[0]),
        pltpu.make_async_copy(d_all, d_out.at[span], row_sem.at[1]),
    ]
    for copy in joined:
        copy.start()

    def kept_copies(p):
        return (
            pltpu.make_async_copy(act_ref.at[p], act_out.at[p, span], out_sem.at[0, p]),
            pltpu.make_async_copy(dpre_ref.at[p], dpre_out.at[p, span], out_sem.at[1, p]),
        )

    def part(p, _):
        pltpu.make_async_copy(ups[0], up_ref.at[p], in_sem.at[0, p]).wait()
        pltpu.make_async_copy(downs[0], down_ref.at[p], in_sem.at[1, p]).wait()
        for r in range(0, rows, STRIP):
            strip = slice(r, r + STRIP)
            up = up_ref[p]
            pre = dot(x_all[strip], up)
            d_act = dot(d_all[strip], down_ref[p], 1, 1)
            sq = pre * pre
            th = jnp.tanh(pre * (GELU_C + (GELU_C * GELU_A) * sq))
            half = 0.5 + 0.5 * th
            act_ref[p, strip] = (pre * half).astype(BF)
            slope = half + (0.5 * pre) * (1.0 - th * th) * (GELU_C + (3.0 * GELU_C * GELU_A) * sq)
            d_pre = (d_act * slope).astype(BF)
            dpre_ref[p, strip] = d_pre
            acc_ref[strip] += dot(d_pre, up, 1, 1)
        for copy in kept_copies(p):
            copy.start()
        return 0

    lax.fori_loop(0, parts, part, 0)
    for e in range(groups):
        results[e][...] = acc_ref[e * rows_each : (e + 1) * rows_each].astype(BF)
    for copy in joined:
        copy.wait()
    for p in range(parts):
        for copy in kept_copies(p):
            copy.wait()


def experts(scal, ups, downs, xs, d_rows, first_row, members, direct, kept):
    width, units = ups[0].shape
    parts, groups = len(ups), len(xs)
    rows_each = xs[0].shape[0]
    rows = groups * rows_each
    total = d_rows.shape[0] * d_rows.shape[1]
    inputs = 1 + 2 * parts + groups + 1
    flat = pl.pallas_call(
        functools.partial(expert_kernel, groups, rows_each, first_row, members, direct, bool(kept)),
        out_shape=[shape((parts, total, units), BF)] * 2
        + [shape((total, width), BF)] * 2
        + [shape((rows_each, width), BF)] * groups,
        in_specs=[pl.BlockSpec(memory_space=pltpu.SMEM)]
        + anywhere(2 * parts)
        + vmem(groups)
        + anywhere(1 + len(kept)),
        out_specs=anywhere(4) + vmem(groups),
        scratch_shapes=[
            pltpu.VMEM((parts, width, units), BF),
            pltpu.VMEM((parts, units, width), BF),
            pltpu.VMEM((parts, rows, units), BF),
            pltpu.VMEM((parts, rows, units), BF),
            pltpu.VMEM((rows, width), BF),
            pltpu.VMEM((rows, width), BF),
            pltpu.VMEM((rows, width), F32),
            pltpu.SemaphoreType.DMA((2, parts)),
            pltpu.SemaphoreType.DMA((groups,)),
            pltpu.SemaphoreType.DMA((2, parts)),
            pltpu.SemaphoreType.DMA((2,)),
        ],
        input_output_aliases={inputs + n: n for n in range(len(kept))},
        compiler_params=params(58),
    )(scal, *ups, *downs, *xs, d_rows, *kept)
    return flat[:4], flat[4:]


def expert_out_kernel(order, rows_each, s_ref, act_ref, *refs):
    downs, out_ref = refs[:-1], refs[-1]
    step = pl.program_id(0)
    total = functools.reduce(jnp.add, [dot(act_ref[p], downs[p][...]) for p in range(4)]).astype(BF)
    if len(order) == 1:
        out_ref[0, pl.ds(pl.multiple_of(step * STRIP, 16), STRIP)] = total
    else:
        each = STRIP // rows_each
        for n in range(len(order) // each):

            @pl.when(step == n)
            def _():
                for m in range(each):
                    out_ref[s_ref[1] ^ order[n * each + m]] = total[m * rows_each : (m + 1) * rows_each]


def expert_out(scal, act, downs, order):
    parts, rows, units = act.shape
    width = downs[0].shape[1]
    rows_each = rows // len(order)
    return pl.pallas_call(
        functools.partial(expert_out_kernel, order, rows_each),
        grid=(rows // STRIP,),
        out_shape=shape((len(order), rows_each, width), BF),
        in_specs=[
            pl.BlockSpec(memory_space=pltpu.SMEM),
            pl.BlockSpec((parts, STRIP, units), lambda n: (0, n, 0)),
        ]
        + [pl.BlockSpec((units, width), lambda n: (0, 0))] * parts,
        out_specs=pl.BlockSpec((len(order), rows_each, width), lambda n: (0, 0, 0)),
        compiler_params=params(58),
    )(scal, act, *downs)


def expert_grad_kernel(left_ref, right_ref, *refs):
    outs, (turned, result, sem) = refs[:4], refs[4:]
    step = pl.program_id(0)

    @pl.when(step == 0)
    def _():
        turned[...] = left_ref[...].T

    result[step] = dot(turned[...], right_ref[0]).astype(BF)
    copies = [pltpu.make_async_copy(result.at[n], outs[3 - n], sem.at[n]) for n in range(4)]
    for n in range(4):

        @pl.when(step == n)
        def _():
            copies[n].start()

    @pl.when(step == 3)
    def _():
        for copy in copies:
            copy.wait()


def expert_grads(left, right):
    rows, width = left.shape
    units = right.shape[2]
    return pl.pallas_call(
        expert_grad_kernel,
        grid=(4,),
        out_shape=[shape((width, units), BF)] * 4,
        in_specs=[
            pl.BlockSpec((rows, width), lambda n: (0, 0)),
            pl.BlockSpec((1, rows, units), lambda n: (3 - n, 0, 0)),
        ],
        out_specs=anywhere(4),
        scratch_shapes=[
            pltpu.VMEM((width, rows), BF),
            pltpu.VMEM((4, width, units), BF),
            pltpu.SemaphoreType.DMA((4,)),
        ],
        compiler_params=params(58),
    )(left, right)


def finish_kernel(x_ref, p0, r0, r2, gain, dh_ref, out_ref):
    d = p0[...].astype(F32) + r0[...].astype(F32) + r2[...].astype(F32)
    x = x_ref[...].astype(F32)
    r = lax.rsqrt(jnp.mean(x * x, -1, keepdims=True) + EPS)
    u = x * r
    gd = gain[...] * d
    out_ref[...] = dh_ref[...] + r * (gd - u * jnp.mean(u * gd, -1, keepdims=True))


def finish_input(x, p0, r0, r2, gain, d_hidden):
    rows, width = x.shape
    strip = pl.BlockSpec((rows // 4, width), lambda n: (n, 0))
    return pl.pallas_call(
        finish_kernel,
        grid=(4,),
        out_shape=shape(x.shape, F32),
        in_specs=[strip] * 4 + [pl.BlockSpec((1, width), lambda n: (0, 0)), strip],
        out_specs=strip,
        compiler_params=params(),
    )(x, p0, r0, r2, gain, d_hidden)


def exchange(value):
    count = lax.axis_size(EX)
    parts = value.reshape(count, -1, value.shape[-1])
    return lax.all_to_all(parts, EX, 0, 0, tiled=True)


def add_low(*parts):
    return functools.reduce(jnp.add, [part.astype(F32) for part in parts]).astype(BF)


def sum_expert(value):
    me = lax.axis_index(EX)
    count = lax.axis_size(EX)
    bits = []
    bit = 1
    while bit < count:
        half = value.shape[0] // 2
        mine = (me & bit) > 0
        keep = jnp.where(mine, value[half:], value[:half])
        give = jnp.where(mine, value[:half], value[half:]).astype(BF)
        value = keep + swap(give, EX, bit).astype(F32)
        bits.append(bit)
        bit *= 2
    value = value.astype(BF)
    for bit in reversed(bits):
        mine = (me & bit) > 0
        other = swap(value, EX, bit)
        value = jnp.concatenate(
            [jnp.where(mine, other, value), jnp.where(mine, value, other)], 0
        )
    return value.astype(F32)


def sum_small(value, axis):
    bit = 1
    while bit < lax.axis_size(axis):
        value = value + swap(value, axis, bit)
        bit *= 2
    return value


def on_device(
    layer_input,
    segment_ids,
    routes,
    gate_values,
    attn_gain,
    qkv_weight,
    position_bias,
    out_weight,
    moe_gain,
    up_weight,
    down_weight,
    out_grad,
):
    rows, width = layer_input.shape
    heads, buckets = position_bias.shape
    loc = qkv_weight.shape[2]
    size = loc // heads
    lanes = lax.axis_size(EX)
    experts_all = up_weight.shape[0] * lanes
    capacity = rows * routes.shape[1] * 5 // (4 * experts_all)
    direct = lanes == 8
    groups = lanes if direct else 1
    rows_each = experts_all * capacity // groups
    t = lax.axis_index(TE)
    me = lax.axis_index(EX)
    scal = jnp.stack([t, me]).astype(jnp.int32)
    gain_one = attn_gain.reshape(1, width)
    gain_two = moe_gain.reshape(1, width)
    turned = jnp.swapaxes(qkv_weight, 1, 2)
    scale = size**-0.5

    far_x = swap(layer_input, TE, 2)
    near_x = swap(layer_input, TE, 1)
    counts = jnp.sum(
        (segment_ids.reshape(-1, 1) < jnp.arange(1, 129, dtype=jnp.int32)[None, :]).astype(jnp.int32), 0
    )
    counts = sum_small(jnp.broadcast_to(counts[None, :], (8, 128)), TE)
    last_x = swap(far_x, TE, 1)
    kept = project(0, (layer_input, near_x), gain_one, turned, scale, [])
    norm, k, qt, vt = project(4, (far_x, last_x), gain_one, turned, scale, kept)

    slot_rows, slot_cols, gates, d_send = send_grad(
        scal, routes.T, gate_values.T, out_grad, experts_all, capacity, direct
    )
    d_rows = exchange(d_send).reshape(groups, rows_each, width)

    up, down = up_weight[0], down_weight[0]
    up_near = swap(up, TE, 1)
    down_near = swap(down, TE, 1)
    up_far = swap(up, TE, 2)
    up_last = swap(up_far, TE, 1)
    down_far = swap(down, TE, 2)
    down_last = swap(down_far, TE, 1)
    ups = (up, up_near, up_far, up_last)
    downs = (down, down_near, down_far, down_last)

    last = position_bias[:, buckets - 1 :]
    column = bucket_index(jnp.arange(TILE, dtype=jnp.int32), buckets)
    column_map = (column[:, None] == jnp.arange(buckets, dtype=jnp.int32)[None, :]).astype(F32)
    line = jnp.dot(position_bias - last, column_map.T, precision=lax.Precision.HIGHEST)
    line = jnp.pad(line, ((0, 8 - heads), (0, 0)))
    common = (scal, counts, k, qt, vt, line, out_weight)
    mix, lse, far_part, give_part = attn_fwd(4, *common, [], heads, size)
    got_far = swap(add_low(far_part, swap(give_part, TE, 1)), TE, 2)
    mix, lse, own_part, give_part = attn_fwd(0, *common, [mix, lse], heads, size)
    got_near = swap(give_part, TE, 1)
    q, v, kt = project_again(norm, turned, scale)

    hidden, *sent = send_rows(
        slot_rows, layer_input, own_part, got_near, got_far, gain_two, groups, rows_each
    )
    if direct:
        xs = sent[:1] + [swap(sent[e], EX, e) for e in range(1, groups)]
        chunks = ((4, 5, 2, 3), (0, 1, 6, 7))
    else:
        xs = [exchange(sent[0]).reshape(rows_each, width)]
        chunks = ((0,),)
    order = tuple(e for chunk in chunks for e in chunk)
    kept = []
    back = [None] * groups
    first_row = 0
    for chunk in chunks:
        kept, d_in = experts(scal, ups, downs, [xs[e] for e in chunk], d_rows, first_row, chunk, direct, kept)
        first_row += len(chunk) * rows_each
        for e, block in zip(chunk, d_in):
            back[e] = swap(block, EX, e) if e else block
    if not direct:
        back = [exchange(back[0]).reshape(rows_each, width)]
    act, d_pre, x_all, d_all = kept

    up0, up1, up2, up3 = expert_grads(x_all, d_pre)
    down0, down1, down2, down3 = expert_grads(d_all, act)
    out_rows = exchange(expert_out(scal, act, downs, order))

    def gather_grad(near, far, cross):
        near = swap(near, TE, 1)
        cross = swap(cross, TE, 1)
        return near, swap(add_low(far, cross), TE, 2)

    near, far = gather_grad(up1, up2, up3)
    up_grad = (up0.astype(F32) + near.astype(F32) + far.astype(F32))[None]
    near, far = gather_grad(down1, down2, down3)
    down_grad = turn_sum(down0, near, far)[None]

    d_hidden, d_attn, moe_part = combine_bwd(slot_cols, hidden, gain_two, out_grad, back)
    far_d = swap(d_attn, TE, 2)
    near_d = swap(d_attn, TE, 1)
    last_d = swap(far_d, TE, 1)
    common = (scal, counts, k, v, kt, qt, q)
    rest = (mix, lse, line, out_weight)
    dq, *sums = attn_bwd(0, *common, (d_attn, near_d), *rest, [], heads, size)
    dq, dk, dv, g_line = attn_bwd(4, *common, (far_d, last_d), *rest, sums + [dq], heads, size)
    far_part, give_part = norm_part(4, dq, dk, dv, turned)
    got_far = swap(add_low(far_part, swap(give_part, TE, 1)), TE, 2)
    own_part, give_part = norm_part(0, dq, dk, dv, turned)
    got_near = swap(give_part, TE, 1)
    out_part = out_grads(mix, (d_attn, near_d, far_d, last_d))
    grads = proj_grads(
        scal, dq, dk, dv, norm, turned, out_part, g_line, moe_part, gain_one, lanes if direct else 1, heads
    )
    if direct:
        pairs = [add_low(grads[2 * j], swap(grads[2 * j + 1], EX, 1)) for j in range(4)]
        mine, small = sum_grads([pairs[0]] + [swap(pairs[j], EX, 2 * j) for j in range(1, 4)])
        column_of = [mine] + [swap(mine, EX, 2 * j) for j in range(1, 4)]
        parts = []
        for part in column_of:
            parts += [part, swap(part, EX, 1)]
        proj_sum, out_weight_grad = unpack_grads(scal, parts, loc)
    else:
        small = sum_small(grads[1], EX)
        grads = sum_expert(grads[0])
        proj_sum, out_weight_grad = grads[: 3 * loc], grads[3 * loc :]
    qkv_grad = jnp.swapaxes(proj_sum.reshape(3, loc, width), 1, 2)

    gains = sum_small(small[:8], TE)
    shifted = jnp.roll(column_map, -1, 0)[:, : buckets - 1]
    near_grad = jnp.dot(small[2 : 2 + heads, :TILE], shifted, precision=lax.Precision.HIGHEST)
    position_bias_grad = jnp.concatenate([near_grad, -jnp.sum(near_grad, 1, keepdims=True)], 1)

    layer_output = combine_fwd(slot_cols, gates, hidden, [out_rows.reshape(-1, width)])
    input_grad = finish_input(layer_input, own_part, got_near, got_far, gain_one, d_hidden)
    return (
        layer_output,
        input_grad,
        gains[0],
        qkv_grad,
        position_bias_grad,
        out_weight_grad,
        gains[1],
        up_grad,
        down_grad,
    )


def solution(mesh):
    in_specs = (
        P((EX, TE), None),
        P(EX, TE),
        P((EX, TE), None),
        P((EX, TE), None),
        P(),
        P(None, None, TE),
        P(TE, None),
        P(TE, None),
        P(),
        P(EX, None, TE),
        P(EX, TE, None),
        P((EX, TE), None),
    )
    out_specs = (
        P((EX, TE), None),
        P((EX, TE), None),
        P(),
        P(None, None, TE),
        P(TE, None),
        P(TE, None),
        P(),
        P(EX, None, TE),
        P(EX, TE, None),
    )

    return jax.shard_map(on_device, mesh=mesh, in_specs=in_specs, out_specs=out_specs, check_vma=False)
```

```python
import functools
import math

import jax
import jax.numpy as jnp
from jax import lax
from jax.experimental import pallas as pl
from jax.experimental.pallas import tpu as pltpu
from jax.sharding import PartitionSpec as P


WINDOW = 1024
TILE = 256
STRIP = 320
NEG = -1e30
EPS = 1e-06
BF = jnp.bfloat16
F32 = jnp.float32

EX, TE = "expert", "tensor"
DIAG, PREV, MASK, PLAIN = range(4)


def bucket_edges(buckets):
    half_count = buckets // 2
    edges = list(range(1, half_count))
    for power in range(half_count):
        edges.append(int(math.ceil(half_count * (128.0 / half_count) ** (power / half_count))))
    return edges


def bucket_index(distance, buckets):
    counted = jnp.zeros(distance.shape, jnp.int32)
    for edge in bucket_edges(buckets):
        counted = counted + (distance >= edge).astype(jnp.int32)
    return counted


def dot(left, right, left_dim=1, right_dim=0):
    return lax.dot_general(
        left, right, (((left_dim,), (right_dim,)), ((), ())), preferred_element_type=F32
    )


def swap(value, axis, bit):
    size = lax.axis_size(axis)
    return lax.ppermute(value, axis, [(i, i ^ bit) for i in range(size)])


def vmem(count):
    return [pl.BlockSpec(memory_space=pltpu.VMEM)] * count


def params(mib=56):
    return pltpu.CompilerParams(vmem_limit_bytes=mib << 20)


def anywhere(count):
    return [pl.BlockSpec(memory_space=pl.ANY)] * count


def shape(dims, dtype):
    return jax.ShapeDtypeStruct(dims, dtype)


def proj_kernel(scale, xa_ref, xb_ref, gain, wt_ref, *refs):
    norm, k_ref, qt, vt = refs[-4:]
    x = jnp.where(pl.program_id(0) < 2, xa_ref[...], xb_ref[...]).astype(F32)
    r = lax.rsqrt(jnp.mean(x * x, -1, keepdims=True) + EPS)
    n = (x * r * gain[...]).astype(BF)
    norm[0] = n
    k_ref[0] = dot(n, wt_ref[1], 1, 1).astype(BF)
    qt[0] = (dot(wt_ref[0], n, 1, 1) * scale).astype(BF)
    vt[0] = dot(wt_ref[2], n, 1, 1).astype(BF)


def pair_specs(width):
    return [
        pl.BlockSpec((TILE, width), lambda n: (jnp.minimum(n, 1), 0)),
        pl.BlockSpec((TILE, width), lambda n: (jnp.maximum(n - 2, 0), 0)),
    ]


def project(base, pair, gain, wt, scale, kept):
    width = pair[0].shape[1]
    loc = wt.shape[1]
    dims = ((TILE, width), (TILE, loc), (loc, TILE), (loc, TILE))
    return pl.pallas_call(
        functools.partial(proj_kernel, scale),
        grid=(4,),
        out_shape=[shape((8,) + d, BF) for d in dims],
        in_specs=pair_specs(width)
        + [
            pl.BlockSpec((1, width), lambda n: (0, 0)),
            pl.BlockSpec((3, loc, width), lambda n: (0, 0, 0)),
        ]
        + anywhere(len(kept)),
        out_specs=[pl.BlockSpec((1,) + d, lambda n: (base + n, 0, 0)) for d in dims],
        input_output_aliases={4 + n: n for n in range(len(kept))},
        compiler_params=params(),
    )(*pair, gain, wt, *kept)


def again_kernel(scale, n_ref, wt_ref, q_ref, v_ref, kt_ref):
    n = n_ref[0]
    q_ref[0] = (dot(n, wt_ref[0], 1, 1) * scale).astype(BF)
    v_ref[0] = dot(n, wt_ref[2], 1, 1).astype(BF)
    kt_ref[0] = dot(wt_ref[1], n, 1, 1).astype(BF)


def project_again(norm, wt, scale):
    tiles, _, width = norm.shape
    loc = wt.shape[1]
    nat = pl.BlockSpec((1, TILE, loc), lambda n: (n, 0, 0))
    return pl.pallas_call(
        functools.partial(again_kernel, scale),
        grid=(tiles,),
        out_shape=[shape((tiles, TILE, loc), BF)] * 2 + [shape((tiles, loc, TILE), BF)],
        in_specs=[
            pl.BlockSpec((1, TILE, width), lambda n: (n, 0, 0)),
            pl.BlockSpec((3, loc, width), lambda n: (0, 0, 0)),
        ],
        out_specs=[nat, nat, pl.BlockSpec((1, loc, TILE), lambda n: (n, 0, 0))],
        compiler_params=params(),
    )(norm, wt)


def head_rows(head, size, dims, axis):
    index = lax.broadcasted_iota(jnp.int32, dims, axis)
    return (index >= head * size) & (index < (head + 1) * size)


def first_key(q, c1, c2):
    start = jnp.where(q >= c2, c2, jnp.where(q >= c1, c1, 0))
    return jnp.maximum(start, q - (WINDOW - 1))


def build_bias(line_ref, bias_ref, heads):
    for h in range(heads):
        row = jnp.broadcast_to(line_ref[h : h + 1, :], (TILE, TILE))
        bias_ref[h] = pltpu.roll(row, 0, 1, stride=1, stride_axis=0)


def key_loop(i, c1, c2, tiles):
    start = first_key(i * TILE, c1, c2) // TILE
    full = (first_key(i * TILE + TILE - 1, c1, c2) + TILE - 1) // TILE
    carry = tiles([(i, DIAG), (i - 1, PREV)], None)
    count = jnp.maximum(i - 1 - start, 0)
    plain = jnp.minimum(jnp.maximum(i - 1 - full, 0), count)
    carry = lax.fori_loop(0, plain, lambda n, c: tiles([(i - 2 - n, PLAIN)], c), carry)
    return lax.fori_loop(plain, count, lambda n, c: tiles([(i - 2 - n, MASK)], c), carry)


def tile_masks(tiles, low, t):
    kk = lax.broadcasted_iota(jnp.int32, (TILE, TILE), 0)
    qq = lax.broadcasted_iota(jnp.int32, (TILE, TILE), 1)
    out = []
    for j, kind in tiles:
        ok = None
        if kind != PLAIN:
            ok = kk >= low - j * TILE
            if kind == DIAG:
                ok = ok & (kk <= qq)
        out.append((jnp.maximum(j, 0) ^ (2 * t), kind, ok))
    return out, qq < kk


def add_bias(s, kind, bias, wrapped):
    if kind == DIAG:
        return s + bias
    if kind == PREV:
        return s + jnp.where(wrapped, bias, 0.0)
    return s


def attn_fwd_kernel(heads, size, base, s_ref, c_ref, k_ref, qt_ref, vt_ref, line_ref, wo_ref, *refs):
    mix_ref, lse_ref, pa_ref, pb_ref, bias_ref = refs[-5:]
    t, c1, c2 = s_ref[0], c_ref[0, 0], c_ref[0, 1]
    loc = heads * size
    step = pl.program_id(0)

    @pl.when(step == 0)
    def _():
        build_bias(line_ref, bias_ref, heads)

    i = (base + step) ^ (2 * t)
    qt = qt_ref[0]
    zero = jnp.zeros_like(qt)
    qz = [jnp.where(head_rows(h, size, (loc, TILE), 0), qt, zero) for h in range(heads)]
    qpos = i * TILE + lax.broadcasted_iota(jnp.int32, (1, TILE), 1)
    low = first_key(qpos, c1, c2)

    def tiles(pairs, carry):
        pairs, wrapped = tile_masks(pairs, low, t)
        scores = []
        for h in range(heads):
            for at, kind, ok in pairs:
                s = add_bias(dot(k_ref[at], qz[h]), kind, bias_ref[h], wrapped)
                scores.append(s if ok is None else jnp.where(ok, s, NEG))
        out = []
        for h in range(heads):
            mine = scores[h * len(pairs) : (h + 1) * len(pairs)]
            m = functools.reduce(jnp.maximum, mine)
            m = jnp.max(m, 0, keepdims=True)
            if carry is not None:
                m = jnp.maximum(carry[h][0], m)
            probs = [jnp.exp(s - m) for s in mine]
            total = jnp.sum(functools.reduce(jnp.add, probs), 0, keepdims=True)
            acc = None
            for (at, _, _), p in zip(pairs, probs):
                piece = dot(vt_ref[at][h * size : (h + 1) * size], p.astype(BF))
                acc = piece if acc is None else acc + piece
            if carry is not None:
                decay = jnp.exp(carry[h][0] - m)
                total = decay * carry[h][1] + total
                acc = decay * carry[h][2] + acc
            out.append((m, total, acc))
        return tuple(out)

    final = key_loop(i, c1, c2, tiles)
    mixed = []
    for h in range(heads):
        m, total, acc = final[h]
        mixed.append((acc * (1.0 / total)).astype(BF))
        lse_ref[0, h : h + 1, :] = m + jnp.log(total)
    mixed = jnp.concatenate(mixed, 0)
    mix_ref[0] = mixed
    part = dot(mixed, wo_ref[...], 0, 0).astype(BF)

    @pl.when(step < 2)
    def _():
        pa_ref[...] = part

    @pl.when(step >= 2)
    def _():
        pb_ref[...] = part


def attn_fwd(base, scal, counts, k, qt, vt, line, wo, kept, heads, size):
    tiles, _, loc = k.shape
    width = wo.shape[1]
    tile = lambda n: (base + n, 0, 0)
    return pl.pallas_call(
        functools.partial(attn_fwd_kernel, heads, size, base),
        grid=(4,),
        out_shape=(
            shape((tiles, loc, TILE), BF),
            shape((tiles, 8, TILE), F32),
            shape((2 * TILE, width), BF),
            shape((2 * TILE, width), BF),
        ),
        in_specs=[
            pl.BlockSpec(memory_space=pltpu.SMEM),
            pl.BlockSpec(memory_space=pltpu.SMEM),
            pl.BlockSpec((tiles, TILE, loc), lambda n: (0, 0, 0)),
            pl.BlockSpec((1, loc, TILE), tile),
            pl.BlockSpec((tiles, loc, TILE), lambda n: (0, 0, 0)),
            pl.BlockSpec((8, TILE), lambda n: (0, 0)),
            pl.BlockSpec((loc, width), lambda n: (0, 0)),
        ]
        + anywhere(len(kept)),
        out_specs=(
            pl.BlockSpec((1, loc, TILE), tile),
            pl.BlockSpec((1, 8, TILE), tile),
            *pair_specs(width),
        ),
        scratch_shapes=[pltpu.VMEM((heads, TILE, TILE), F32)],
        input_output_aliases={7 + n: n for n in range(len(kept))},
        compiler_params=params(),
    )(scal, counts, k, qt, vt, line, wo, *kept)


def attn_bwd_kernel(
    heads,
    size,
    base,
    last,
    s_ref,
    c_ref,
    k_ref,
    v_ref,
    kt_ref,
    qt_ref,
    q_ref,
    da_ref,
    db_ref,
    mix_ref,
    lse_ref,
    line_ref,
    wo_ref,
    *refs,
):
    bias_ref = refs[-1]
    if last:
        dq_near, dk_in, dv_in, g_in, og_in, moe_ref, gain_ref, norm_ref, wt_ref = refs[:9]
        part_refs, outs = refs[9:13], refs[13:-8]
        dq_ref, dk_ref, dv_ref, g_ref, og_ref, sum_ref, small_ref = refs[-8:-1]
    else:
        dq_ref, dk_ref, dv_ref, g_ref, og_ref = refs[:-1]
    t, c1, c2 = s_ref[0], c_ref[0, 0], c_ref[0, 1]
    loc = heads * size
    step = pl.program_id(0)

    @pl.when(step == 0)
    def _():
        build_bias(line_ref, bias_ref, heads)
        if last:
            dk_ref[...] = dk_in[...]
            dv_ref[...] = dv_in[...]
            g_ref[...] = g_in[...]
            og_ref[...] = og_in[...]
        else:
            dk_ref[...] = jnp.zeros_like(dk_ref)
            dv_ref[...] = jnp.zeros_like(dv_ref)
            g_ref[...] = jnp.zeros_like(g_ref)
            og_ref[...] = jnp.zeros_like(og_ref)

    i = (base + step) ^ (2 * t)
    rows = jnp.where(step < 2, da_ref[...], db_ref[...])
    dn = dot(rows, wo_ref[...], 1, 1).astype(BF)
    dt = dot(wo_ref[...], rows, 1, 1).astype(BF)
    og_ref[...] += dot(mix_ref[0], rows)
    qt = qt_ref[0]
    qn = q_ref[0]
    zt = jnp.zeros_like(qt)
    zn = jnp.zeros_like(qn)
    rh = [head_rows(h, size, (loc, TILE), 0) for h in range(heads)]
    ch = [head_rows(h, size, (TILE, loc), 1) for h in range(heads)]
    qz = [jnp.where(rh[h], qt, zt) for h in range(heads)]
    dz = [jnp.where(rh[h], dt, zt) for h in range(heads)]
    qm = [jnp.where(ch[h], qn, zn) for h in range(heads)]
    dm = [jnp.where(ch[h], dn, zn) for h in range(heads)]
    prod = dt.astype(F32) * mix_ref[0].astype(F32)
    delta = [jnp.sum(prod[h * size : (h + 1) * size], 0, keepdims=True) for h in range(heads)]
    lse = [lse_ref[0, h : h + 1, :] for h in range(heads)]
    qpos = i * TILE + lax.broadcasted_iota(jnp.int32, (1, TILE), 1)
    low = first_key(qpos, c1, c2)

    def tiles(pairs, carry):
        pairs, wrapped = tile_masks(pairs, low, t)
        out = [None] * heads if carry is None else list(carry)
        raw = [[(dot(k_ref[at], qz[h]), dot(v_ref[at], dz[h])) for h in range(heads)] for at, _, _ in pairs]
        narrow = []
        for (at, kind, ok), products in zip(pairs, raw):
            lows = []
            for h, (s, dp) in enumerate(products):
                s = add_bias(s, kind, bias_ref[h], wrapped) - lse[h]
                if ok is not None:
                    s = jnp.where(ok, s, NEG)
                p = jnp.exp(s)
                ds = p * (dp - delta[h])
                if kind == DIAG:
                    g_ref[h] += ds
                elif kind == PREV:
                    g_ref[h] += jnp.where(wrapped, ds, 0.0)
                lows.append((p.astype(BF), ds.astype(BF)))
            narrow.append(lows)
        for (at, _, _), lows in zip(pairs, narrow):
            dv = None
            dk = None
            for h, (p, ds) in enumerate(lows):
                piece = dot(p, dm[h])
                dv = piece if dv is None else dv + piece
                piece = dot(ds, qm[h])
                dk = piece if dk is None else dk + piece
                piece = dot(kt_ref[at][h * size : (h + 1) * size], ds)
                out[h] = piece if out[h] is None else out[h] + piece
            dv_ref[at] += dv
            dk_ref[at] += dk
        return tuple(out)

    final = key_loop(i, c1, c2, tiles)
    dq = (jnp.concatenate(final, 0) * (size**-0.5)).astype(BF)
    if not last:
        dq_ref[...] = dq
        return
    dq_ref[:, pl.ds(pl.multiple_of(step * TILE, TILE), TILE)] = dq

    @pl.when(step == pl.num_programs(0) - 1)
    def _():
        tokens = norm_ref.shape[0]
        each = tokens // 4
        dk = dk_ref[...].astype(BF).reshape(tokens, loc)
        dv = dv_ref[...].astype(BF).reshape(tokens, loc)
        near, far = dq_near[...], dq_ref[...]
        sum_ref[0:loc] = dot(near, norm_ref[0 : 2 * each]) + dot(far, norm_ref[2 * each : tokens])
        sum_ref[loc : 2 * loc] = dot(dk, norm_ref[...], 0, 0)
        sum_ref[2 * loc : 3 * loc] = dot(dv, norm_ref[...], 0, 0)
        sum_ref[3 * loc : 4 * loc] = og_ref[...]
        for pos, part_ref in enumerate(part_refs):
            mine = (near, far)[pos // 2][:, (pos % 2) * each : (pos % 2 + 1) * each]
            span = slice(pos * each, (pos + 1) * each)
            part = dot(mine, wt_ref[0], 0, 0) + dot(dk[span], wt_ref[1]) + dot(dv[span], wt_ref[2])
            part_ref[...] = part.astype(BF)
        total = None
        for c in range(3):
            line = jnp.sum(sum_ref[c * loc : (c + 1) * loc] * wt_ref[c].astype(F32), 0, keepdims=True)
            total = line if total is None else total + line
        small_ref[...] = jnp.zeros_like(small_ref)
        small_ref[0:1] = total / gain_ref[...]
        small_ref[1:2] = moe_ref[0:1]
        kk = lax.broadcasted_iota(jnp.int32, (TILE, TILE), 0)
        qq = lax.broadcasted_iota(jnp.int32, (TILE, TILE), 1)
        flip = (kk + qq == TILE - 1).astype(F32)
        for h in range(heads):
            g = lax.dot_general(
                flip,
                g_ref[h],
                (((1,), (0,)), ((), ())),
                precision=lax.Precision.HIGHEST,
                preferred_element_type=F32,
            )
            g = pltpu.roll(g, 0, 1, stride=1, stride_axis=0)
            small_ref[2 + h : 3 + h, 0:TILE] = jnp.sum(g, 0, keepdims=True)
        if len(outs) == 2:
            outs[0][...] = sum_ref[...]
            outs[1][...] = small_ref[...]
        else:
            count = 4 * loc // len(outs)
            small = small_ref[...].astype(BF)
            for e, out in enumerate(outs):
                first = pl.multiple_of((s_ref[1] ^ e) * count, 16)
                out[0:count] = sum_ref[pl.ds(first, count)].astype(BF)
                out[count : count + 16] = small


def attn_bwd(base, scal, counts, k, v, kt, qt, q, d_rows, mix, lse, line, wo, sums, heads, size, chunks=1):
    tiles, _, loc = k.shape
    width = wo.shape[1]
    last = bool(sums)
    tile = lambda n: (base + n, 0, 0)
    whole = lambda *dims: pl.BlockSpec(dims, lambda n: (0,) * len(dims))
    nat = whole(tiles, TILE, loc)
    square = whole(heads, TILE, TILE)
    half = tiles // 2 * TILE
    in_specs = [
        pl.BlockSpec(memory_space=pltpu.SMEM),
        pl.BlockSpec(memory_space=pltpu.SMEM),
        nat,
        nat,
        whole(tiles, loc, TILE),
        pl.BlockSpec((1, loc, TILE), tile),
        pl.BlockSpec((1, TILE, loc), tile),
        *pair_specs(width),
        pl.BlockSpec((1, loc, TILE), tile),
        pl.BlockSpec((1, 8, TILE), tile),
        whole(8, TILE),
        whole(loc, width),
    ]
    running = [(tiles, TILE, loc)] * 2 + [(heads, TILE, TILE), (loc, width)]
    if last:
        in_specs += [whole(loc, half), nat, nat, square, whole(loc, width), whole(8, width), whole(1, width)]
        in_specs += [whole(2 * half, width), whole(3, loc, width)]
        results = [((half // 2, width), BF)] * 4
        if chunks == 1:
            results += [((4 * loc, width), F32), ((16, width), F32)]
        else:
            results += [((4 * loc // chunks + 16, width), BF)] * chunks
        out_specs = [whole(*dims) for dims, _ in results]
        scratch = [pltpu.VMEM((loc, half), BF)] + [pltpu.VMEM(dims, F32) for dims in running]
        scratch += [pltpu.VMEM((4 * loc, width), F32), pltpu.VMEM((16, width), F32)]
    else:
        results = [((loc, half), BF)] + [(dims, F32) for dims in running]
        out_specs = [pl.BlockSpec((loc, TILE), lambda n: (0, n))] + [whole(*dims) for dims in running]
        scratch = []
    return pl.pallas_call(
        functools.partial(attn_bwd_kernel, heads, size, base, last),
        grid=(4,),
        out_shape=[shape(dims, kind) for dims, kind in results],
        in_specs=in_specs,
        out_specs=out_specs,
        scratch_shapes=scratch + [pltpu.VMEM((heads, TILE, TILE), F32)],
        compiler_params=params(),
    )(scal, counts, k, v, kt, qt, q, *d_rows, mix, lse, line, wo, *sums)


def sum_grads_kernel(*refs):
    parts, (out_ref, small_ref) = refs[:-2], refs[-2:]
    total = functools.reduce(jnp.add, [part[...].astype(F32) for part in parts])
    rows = out_ref.shape[0]
    out_ref[...] = total[0:rows].astype(BF)
    small_ref[...] = total[rows:]


def sum_grads(parts):
    rows, width = parts[0].shape
    return pl.pallas_call(
        sum_grads_kernel,
        out_shape=[shape((rows - 16, width), BF), shape((16, width), F32)],
        in_specs=vmem(len(parts)),
        out_specs=vmem(2),
        compiler_params=params(),
    )(*parts)


def unpack_kernel(s_ref, *refs):
    parts, (proj_ref, out_ref) = refs[:-2], refs[-2:]
    rows = parts[0].shape[0]
    edge = proj_ref.shape[0] // rows
    for e, part in enumerate(parts):
        at = s_ref[1] ^ e

        @pl.when(at < edge)
        def _():
            proj_ref[pl.ds(pl.multiple_of(at * rows, 16), rows)] = part[...].astype(F32)

        @pl.when(at >= edge)
        def _():
            out_ref[pl.ds(pl.multiple_of((at - edge) * rows, 16), rows)] = part[...].astype(F32)


def unpack_grads(scal, parts, loc):
    width = parts[0].shape[1]
    return pl.pallas_call(
        unpack_kernel,
        out_shape=[shape((3 * loc, width), F32), shape((loc, width), F32)],
        in_specs=[pl.BlockSpec(memory_space=pltpu.SMEM)] + vmem(len(parts)),
        out_specs=vmem(2),
        compiler_params=params(),
    )(scal, *parts)


def turn_sum_kernel(a_ref, b_ref, c_ref, out_ref):
    out_ref[...] = (a_ref[...].astype(F32) + b_ref[...].astype(F32) + c_ref[...].astype(F32)).T


def turn_sum(a, b, c):
    return pl.pallas_call(
        turn_sum_kernel,
        grid=(3,),
        out_shape=shape(a.shape[::-1], F32),
        in_specs=[pl.BlockSpec((a.shape[0], a.shape[1] // 3), lambda n: (0, n))] * 3,
        out_specs=pl.BlockSpec((a.shape[1] // 3, a.shape[0]), lambda n: (n, 0)),
        compiler_params=params(),
    )(a, b, c)


def select_rows(slot_rows, first, count, ranks):
    want = first + lax.broadcasted_iota(jnp.int32, (count, slot_rows.shape[1]), 0)
    return [(slot_rows[r : r + 1, :] == want).astype(BF) for r in ranks]


def send_grad_kernel(
    experts_all, capacity, direct, s_ref, route_ref, gate_ref, grad_ref, rows_ref, cols_ref, gcol_ref, out_ref
):
    tokens = route_ref.shape[1]
    expert = lax.broadcasted_iota(jnp.int32, (max(8, experts_all), tokens), 0)
    hit = [route_ref[r : r + 1, :] == expert for r in range(2)]
    both = hit[0].astype(BF) + hit[1].astype(BF)
    first = lax.broadcasted_iota(jnp.int32, (tokens, tokens), 0)
    later = lax.broadcasted_iota(jnp.int32, (tokens, tokens), 1)
    earlier = dot(both, (first < later).astype(BF))
    rows = []
    for mask in (0, s_ref[1] if direct else 0):
        for r in range(2):
            place = jnp.sum(jnp.where(hit[r], earlier, 0.0), 0, keepdims=True).astype(jnp.int32)
            slot = (route_ref[r : r + 1, :] ^ mask) * capacity + place
            rows.append(jnp.where(place < capacity, slot, -1))
    rows = jnp.concatenate(rows + rows, 0)
    rows_ref[...] = rows
    cols_ref[...] = rows.astype(F32).T.astype(jnp.int32)
    gates = jnp.concatenate([gate_ref[...]] * 4, 0).T
    gcol_ref[...] = gates
    grad = grad_ref[...].astype(F32)
    scaled = [(grad * gates[:, r : r + 1]).astype(BF) for r in range(2)]

    def strip(n, _):
        first = pl.multiple_of(n * STRIP, 16)
        hot = select_rows(rows_ref, first, STRIP, (0, 1))
        out_ref[pl.ds(first, STRIP)] = (dot(hot[0], scaled[0]) + dot(hot[1], scaled[1])).astype(BF)
        return 0

    lax.fori_loop(0, out_ref.shape[0] // STRIP, strip, 0)


def send_grad(scal, routes, gates, grad, experts_all, capacity, direct):
    tokens, width = grad.shape
    return pl.pallas_call(
        functools.partial(send_grad_kernel, experts_all, capacity, direct),
        out_shape=[
            shape((8, tokens), jnp.int32),
            shape((tokens, 8), jnp.int32),
            shape((tokens, 8), F32),
            shape((experts_all * capacity, width), BF),
        ],
        in_specs=[pl.BlockSpec(memory_space=pltpu.SMEM)] + vmem(3),
        out_specs=vmem(4),
        compiler_params=params(),
    )(scal, routes, gates, grad)


def send_rows_kernel(rows_each, slot_ref, x_ref, p0, r0, r2, gain, hid_ref, *refs):
    outs, joined = refs[:-1], refs[-1]
    attn = p0[...].astype(F32) + r0[...].astype(F32) + r2[...].astype(F32)
    hidden = x_ref[...].astype(F32) + attn
    hid_ref[...] = hidden
    r = lax.rsqrt(jnp.mean(hidden * hidden, -1, keepdims=True) + EPS)
    norm = (hidden * r * gain[...]).astype(BF)

    def strip(n, _):
        first = pl.multiple_of(n * STRIP, 16)
        hot = select_rows(slot_ref, first, STRIP, (2, 3))
        joined[pl.ds(first, STRIP)] = dot(hot[0] + hot[1], norm).astype(BF)
        return 0

    lax.fori_loop(0, joined.shape[0] // STRIP, strip, 0)
    for e, out in enumerate(outs):
        out[...] = joined[e * rows_each : (e + 1) * rows_each]


def send_rows(slot_rows, x, p0, r0, r2, gain, groups, rows_each):
    rows, width = x.shape
    return pl.pallas_call(
        functools.partial(send_rows_kernel, rows_each),
        out_shape=[shape((rows, width), F32)] + [shape((rows_each, width), BF)] * groups,
        in_specs=vmem(6),
        out_specs=vmem(1 + groups),
        scratch_shapes=[pltpu.VMEM((groups * rows_each, width), BF)],
        compiler_params=params(),
    )(slot_rows, x, p0, r0, r2, gain)


TOKENS = 128


def picks(slot_ref, first, base, slots):
    own = slot_ref[pl.ds(first, TOKENS), :]
    at = lax.broadcasted_iota(jnp.int32, (TOKENS, slots), 1)
    return [(own[:, base + r : base + r + 1] == at).astype(BF) for r in range(2)]


def combine_bwd_kernel(groups, slot_ref, hid_ref, gain, grad_ref, *refs):
    blocks, (dh_ref, da_ref, gg_ref, joined) = refs[:groups], refs[groups:]
    at = 0
    for block in blocks:
        joined[at : at + block.shape[0]] = block[...]
        at += block.shape[0]
    gg_ref[...] = jnp.zeros_like(gg_ref)

    def strip(n, _):
        first = pl.multiple_of(n * TOKENS, TOKENS)
        span = pl.ds(first, TOKENS)
        hot = picks(slot_ref, first, 2, joined.shape[0])
        d = dot(hot[0] + hot[1], joined[...])
        hidden = hid_ref[span]
        r = lax.rsqrt(jnp.mean(hidden * hidden, -1, keepdims=True) + EPS)
        u = hidden * r
        gg_ref[...] += jnp.sum(u * d, 0, keepdims=True)
        gd = gain[...] * d
        dv = r * (gd - u * jnp.mean(u * gd, -1, keepdims=True))
        d_hidden = grad_ref[span].astype(F32) + dv
        dh_ref[span] = d_hidden
        da_ref[span] = d_hidden.astype(BF)
        return 0

    lax.fori_loop(0, hid_ref.shape[0] // TOKENS, strip, 0)


def combine_bwd(slot_cols, hidden, gain, grad, blocks):
    rows, width = hidden.shape
    groups = len(blocks)
    return pl.pallas_call(
        functools.partial(combine_bwd_kernel, groups),
        out_shape=(shape((rows, width), F32), shape((rows, width), BF), shape((8, width), F32)),
        in_specs=vmem(4 + groups),
        out_specs=vmem(3),
        scratch_shapes=[pltpu.VMEM((groups * blocks[0].shape[0], width), BF)],
        compiler_params=params(),
    )(slot_cols, hidden, gain, grad, *blocks)


def combine_fwd_kernel(slot_ref, gate_ref, hid_ref, data_ref, out_ref):
    def strip(n, _):
        first = pl.multiple_of(n * TOKENS, TOKENS)
        span = pl.ds(first, TOKENS)
        hot = picks(slot_ref, first, 0, data_ref.shape[0])
        gates = gate_ref[span, :]
        mixture = gates[:, 0:1] * dot(hot[0], data_ref[...]) + gates[:, 1:2] * dot(hot[1], data_ref[...])
        out_ref[span] = (hid_ref[span] + mixture).astype(BF)
        return 0

    lax.fori_loop(0, hid_ref.shape[0] // TOKENS, strip, 0)


def combine_fwd(slot_cols, gates, hidden, data):
    return pl.pallas_call(
        combine_fwd_kernel,
        out_shape=shape(hidden.shape, BF),
        in_specs=vmem(4),
        out_specs=vmem(1)[0],
        compiler_params=params(),
    )(slot_cols, gates, hidden, data)


GELU_C = math.sqrt(2.0 / math.pi)
GELU_A = 0.044715


def expert_kernel(groups, rows_each, first_row, members, direct, kept, s_ref, *refs):
    refs = list(refs)
    take = lambda count: [refs.pop(0) for _ in range(count)]
    parts = 4
    ups, downs, xs = take(parts), take(parts), take(groups)
    (d_in_ref,) = take(1)
    take(4 if kept else 0)
    act_out, dpre_out, x_out, d_out = take(4)
    results = take(groups)
    up_ref, down_ref, act_ref, dpre_ref, x_all, d_all, acc_ref, in_sem, d_sem, out_sem, row_sem = refs
    rows = groups * rows_each
    span = pl.ds(first_row, rows)
    own = []
    for n, e in enumerate(members):
        source = (s_ref[1] ^ e) if direct else 0
        own.append(
            pltpu.make_async_copy(
                d_in_ref.at[source], d_all.at[pl.ds(n * rows_each, rows_each)], d_sem.at[n]
            )
        )
        own[n].start()
    for p in range(parts):
        pltpu.make_async_copy(ups[p], up_ref.at[p], in_sem.at[0, p]).start()
        pltpu.make_async_copy(downs[p], down_ref.at[p], in_sem.at[1, p]).start()
    for e in range(groups):
        x_all[e * rows_each : (e + 1) * rows_each] = xs[e][...]
    acc_ref[...] = jnp.zeros_like(acc_ref)
    for copy in own:
        copy.wait()
    joined = [
        pltpu.make_async_copy(x_all, x_out.at[span], row_sem.at[0]),
        pltpu.make_async_copy(d_all, d_out.at[span], row_sem.at[1]),
    ]
    for copy in joined:
        copy.start()

    def kept_copies(p):
        return (
            pltpu.make_async_copy(act_ref.at[p], act_out.at[p, span], out_sem.at[0, p]),
            pltpu.make_async_copy(dpre_ref.at[p], dpre_out.at[p, span], out_sem.at[1, p]),
        )

    def part(p, _):
        pltpu.make_async_copy(ups[0], up_ref.at[p], in_sem.at[0, p]).wait()
        pltpu.make_async_copy(downs[0], down_ref.at[p], in_sem.at[1, p]).wait()
        for r in range(0, rows, STRIP):
            strip = slice(r, r + STRIP)
            up = up_ref[p]
            pre = dot(x_all[strip], up)
            d_act = dot(d_all[strip], down_ref[p], 1, 1)
            sq = pre * pre
            th = jnp.tanh(pre * (GELU_C + (GELU_C * GELU_A) * sq))
            half = 0.5 + 0.5 * th
            act_ref[p, strip] = (pre * half).astype(BF)
            slope = half + (0.5 * pre) * (1.0 - th * th) * (GELU_C + (3.0 * GELU_C * GELU_A) * sq)
            d_pre = (d_act * slope).astype(BF)
            dpre_ref[p, strip] = d_pre
            acc_ref[strip] += dot(d_pre, up, 1, 1)
        for copy in kept_copies(p):
            copy.start()
        return 0

    lax.fori_loop(0, parts, part, 0)
    for e in range(groups):
        results[e][...] = acc_ref[e * rows_each : (e + 1) * rows_each].astype(BF)
    for copy in joined:
        copy.wait()
    for p in range(parts):
        for copy in kept_copies(p):
            copy.wait()


def experts(scal, ups, downs, xs, d_rows, first_row, members, direct, kept):
    width, units = ups[0].shape
    parts, groups = len(ups), len(xs)
    rows_each = xs[0].shape[0]
    rows = groups * rows_each
    total = d_rows.shape[0] * d_rows.shape[1]
    inputs = 1 + 2 * parts + groups + 1
    flat = pl.pallas_call(
        functools.partial(expert_kernel, groups, rows_each, first_row, members, direct, bool(kept)),
        out_shape=[shape((parts, total, units), BF)] * 2
        + [shape((total, width), BF)] * 2
        + [shape((rows_each, width), BF)] * groups,
        in_specs=[pl.BlockSpec(memory_space=pltpu.SMEM)]
        + anywhere(2 * parts)
        + vmem(groups)
        + anywhere(1 + len(kept)),
        out_specs=anywhere(4) + vmem(groups),
        scratch_shapes=[
            pltpu.VMEM((parts, width, units), BF),
            pltpu.VMEM((parts, units, width), BF),
            pltpu.VMEM((parts, rows, units), BF),
            pltpu.VMEM((parts, rows, units), BF),
            pltpu.VMEM((rows, width), BF),
            pltpu.VMEM((rows, width), BF),
            pltpu.VMEM((rows, width), F32),
            pltpu.SemaphoreType.DMA((2, parts)),
            pltpu.SemaphoreType.DMA((groups,)),
            pltpu.SemaphoreType.DMA((2, parts)),
            pltpu.SemaphoreType.DMA((2,)),
        ],
        input_output_aliases={inputs + n: n for n in range(len(kept))},
        compiler_params=params(58),
    )(scal, *ups, *downs, *xs, d_rows, *kept)
    return flat[:4], flat[4:]


def expert_out_kernel(order, rows_each, s_ref, act_ref, *refs):
    downs, out_ref = refs[:-1], refs[-1]
    step = pl.program_id(0)
    total = functools.reduce(jnp.add, [dot(act_ref[p], downs[p][...]) for p in range(4)]).astype(BF)
    if len(order) == 1:
        out_ref[0, pl.ds(pl.multiple_of(step * STRIP, 16), STRIP)] = total
    else:
        each = STRIP // rows_each
        for n in range(len(order) // each):

            @pl.when(step == n)
            def _():
                for m in range(each):
                    out_ref[s_ref[1] ^ order[n * each + m]] = total[m * rows_each : (m + 1) * rows_each]


def expert_out(scal, act, downs, order):
    parts, rows, units = act.shape
    width = downs[0].shape[1]
    rows_each = rows // len(order)
    return pl.pallas_call(
        functools.partial(expert_out_kernel, order, rows_each),
        grid=(rows // STRIP,),
        out_shape=shape((len(order), rows_each, width), BF),
        in_specs=[
            pl.BlockSpec(memory_space=pltpu.SMEM),
            pl.BlockSpec((parts, STRIP, units), lambda n: (0, n, 0)),
        ]
        + [pl.BlockSpec((units, width), lambda n: (0, 0))] * parts,
        out_specs=pl.BlockSpec((len(order), rows_each, width), lambda n: (0, 0, 0)),
        compiler_params=params(58),
    )(scal, act, *downs)


def expert_grad_kernel(left_ref, right_ref, *refs):
    outs, (turned, result, sem) = refs[:4], refs[4:]
    step = pl.program_id(0)

    @pl.when(step == 0)
    def _():
        turned[...] = left_ref[...].T

    result[step] = dot(turned[...], right_ref[0]).astype(BF)
    copies = [pltpu.make_async_copy(result.at[n], outs[3 - n], sem.at[n]) for n in range(4)]
    for n in range(4):

        @pl.when(step == n)
        def _():
            copies[n].start()

    @pl.when(step == 3)
    def _():
        for copy in copies:
            copy.wait()


def expert_grads(left, right):
    rows, width = left.shape
    units = right.shape[2]
    return pl.pallas_call(
        expert_grad_kernel,
        grid=(4,),
        out_shape=[shape((width, units), BF)] * 4,
        in_specs=[
            pl.BlockSpec((rows, width), lambda n: (0, 0)),
            pl.BlockSpec((1, rows, units), lambda n: (3 - n, 0, 0)),
        ],
        out_specs=anywhere(4),
        scratch_shapes=[
            pltpu.VMEM((width, rows), BF),
            pltpu.VMEM((4, width, units), BF),
            pltpu.SemaphoreType.DMA((4,)),
        ],
        compiler_params=params(58),
    )(left, right)


def finish_kernel(x_ref, p0, r0, r2, gain, dh_ref, out_ref):
    d = p0[...].astype(F32) + r0[...].astype(F32) + r2[...].astype(F32)
    x = x_ref[...].astype(F32)
    r = lax.rsqrt(jnp.mean(x * x, -1, keepdims=True) + EPS)
    u = x * r
    gd = gain[...] * d
    out_ref[...] = dh_ref[...] + r * (gd - u * jnp.mean(u * gd, -1, keepdims=True))


def finish_input(x, p0, r0, r2, gain, d_hidden):
    rows, width = x.shape
    strip = pl.BlockSpec((rows // 4, width), lambda n: (n, 0))
    return pl.pallas_call(
        finish_kernel,
        grid=(4,),
        out_shape=shape(x.shape, F32),
        in_specs=[strip] * 4 + [pl.BlockSpec((1, width), lambda n: (0, 0)), strip],
        out_specs=strip,
        compiler_params=params(),
    )(x, p0, r0, r2, gain, d_hidden)


def exchange(value):
    count = lax.axis_size(EX)
    parts = value.reshape(count, -1, value.shape[-1])
    return lax.all_to_all(parts, EX, 0, 0, tiled=True)


def add_low(*parts):
    return functools.reduce(jnp.add, [part.astype(F32) for part in parts]).astype(BF)


def sum_expert(value):
    me = lax.axis_index(EX)
    count = lax.axis_size(EX)
    bits = []
    bit = 1
    while bit < count:
        half = value.shape[0] // 2
        mine = (me & bit) > 0
        keep = jnp.where(mine, value[half:], value[:half])
        give = jnp.where(mine, value[:half], value[half:]).astype(BF)
        value = keep + swap(give, EX, bit).astype(F32)
        bits.append(bit)
        bit *= 2
    value = value.astype(BF)
    for bit in reversed(bits):
        mine = (me & bit) > 0
        other = swap(value, EX, bit)
        value = jnp.concatenate(
            [jnp.where(mine, other, value), jnp.where(mine, value, other)], 0
        )
    return value.astype(F32)


def sum_small(value, axis):
    bit = 1
    while bit < lax.axis_size(axis):
        value = value + swap(value, axis, bit)
        bit *= 2
    return value


def on_device(
    layer_input,
    segment_ids,
    routes,
    gate_values,
    attn_gain,
    qkv_weight,
    position_bias,
    out_weight,
    moe_gain,
    up_weight,
    down_weight,
    out_grad,
):
    rows, width = layer_input.shape
    heads, buckets = position_bias.shape
    loc = qkv_weight.shape[2]
    size = loc // heads
    lanes = lax.axis_size(EX)
    experts_all = up_weight.shape[0] * lanes
    capacity = rows * routes.shape[1] * 5 // (4 * experts_all)
    direct = lanes == 8
    groups = lanes if direct else 1
    rows_each = experts_all * capacity // groups
    t = lax.axis_index(TE)
    me = lax.axis_index(EX)
    scal = jnp.stack([t, me]).astype(jnp.int32)
    gain_one = attn_gain.reshape(1, width)
    gain_two = moe_gain.reshape(1, width)
    turned = jnp.swapaxes(qkv_weight, 1, 2)
    scale = size**-0.5

    far_x = swap(layer_input, TE, 2)
    near_x = swap(layer_input, TE, 1)
    counts = jnp.sum(
        (segment_ids.reshape(-1, 1) < jnp.arange(1, 129, dtype=jnp.int32)[None, :]).astype(jnp.int32), 0
    )
    counts = sum_small(jnp.broadcast_to(counts[None, :], (8, 128)), TE)
    last_x = swap(far_x, TE, 1)
    kept = project(0, (layer_input, near_x), gain_one, turned, scale, [])
    norm, k, qt, vt = project(4, (far_x, last_x), gain_one, turned, scale, kept)

    slot_rows, slot_cols, gates, d_send = send_grad(
        scal, routes.T, gate_values.T, out_grad, experts_all, capacity, direct
    )
    d_rows = exchange(d_send).reshape(groups, rows_each, width)

    up, down = up_weight[0], down_weight[0]
    up_near = swap(up, TE, 1)
    down_near = swap(down, TE, 1)
    up_far = swap(up, TE, 2)
    up_last = swap(up_far, TE, 1)
    down_far = swap(down, TE, 2)
    down_last = swap(down_far, TE, 1)
    ups = (up, up_near, up_far, up_last)
    downs = (down, down_near, down_far, down_last)

    last = position_bias[:, buckets - 1 :]
    column = bucket_index(jnp.arange(TILE, dtype=jnp.int32), buckets)
    column_map = (column[:, None] == jnp.arange(buckets, dtype=jnp.int32)[None, :]).astype(F32)
    line = jnp.dot(position_bias - last, column_map.T, precision=lax.Precision.HIGHEST)
    line = jnp.pad(line, ((0, 8 - heads), (0, 0)))
    common = (scal, counts, k, qt, vt, line, out_weight)
    mix, lse, far_part, give_part = attn_fwd(4, *common, [], heads, size)
    got_far = swap(add_low(far_part, swap(give_part, TE, 1)), TE, 2)
    mix, lse, own_part, give_part = attn_fwd(0, *common, [mix, lse], heads, size)
    got_near = swap(give_part, TE, 1)
    q, v, kt = project_again(norm, turned, scale)

    hidden, *sent = send_rows(
        slot_rows, layer_input, own_part, got_near, got_far, gain_two, groups, rows_each
    )
    if direct:
        xs = sent[:1] + [swap(sent[e], EX, e) for e in range(1, groups)]
        chunks = ((4, 0, 1, 2), (5, 6, 3, 7))
    else:
        xs = [exchange(sent[0]).reshape(rows_each, width)]
        chunks = ((0,),)
    order = tuple(e for chunk in chunks for e in chunk)
    kept = []
    back = [None] * groups
    first_row = 0
    for chunk in chunks:
        kept, d_in = experts(scal, ups, downs, [xs[e] for e in chunk], d_rows, first_row, chunk, direct, kept)
        first_row += len(chunk) * rows_each
        for e, block in zip(chunk, d_in):
            back[e] = swap(block, EX, e) if e else block
    if not direct:
        back = [exchange(back[0]).reshape(rows_each, width)]
    act, d_pre, x_all, d_all = kept

    up0, up1, up2, up3 = expert_grads(x_all, d_pre)
    down0, down1, down2, down3 = expert_grads(d_all, act)
    out_rows = exchange(expert_out(scal, act, downs, order))

    def gather_grad(near, far, cross):
        near = swap(near, TE, 1)
        cross = swap(cross, TE, 1)
        return near, swap(add_low(far, cross), TE, 2)

    near, far = gather_grad(up1, up2, up3)
    up_grad = (up0.astype(F32) + near.astype(F32) + far.astype(F32))[None]
    near, far = gather_grad(down1, down2, down3)
    down_grad = turn_sum(down0, near, far)[None]

    d_hidden, d_attn, moe_part = combine_bwd(slot_cols, hidden, gain_two, out_grad, back)
    far_d = swap(d_attn, TE, 2)
    near_d = swap(d_attn, TE, 1)
    last_d = swap(far_d, TE, 1)
    common = (scal, counts, k, v, kt, qt, q)
    rest = (mix, lse, line, out_weight)
    sums = attn_bwd(0, *common, (d_attn, near_d), *rest, [], heads, size)
    flat_norm = norm.reshape(4 * rows, width)
    own_part, give_part, far_part, give_far, *grads = attn_bwd(
        4, *common, (far_d, last_d), *rest, [*sums, moe_part, gain_one, flat_norm, turned], heads, size,
        groups if direct else 1,
    )
    got_far = swap(add_low(far_part, swap(give_far, TE, 1)), TE, 2)
    got_near = swap(give_part, TE, 1)
    if direct:
        pairs = [add_low(grads[2 * j], swap(grads[2 * j + 1], EX, 1)) for j in range(4)]
        mine, small = sum_grads([pairs[0]] + [swap(pairs[j], EX, 2 * j) for j in range(1, 4)])
        column_of = [mine] + [swap(mine, EX, 2 * j) for j in range(1, 4)]
        parts = []
        for part in column_of:
            parts += [part, swap(part, EX, 1)]
        proj_sum, out_weight_grad = unpack_grads(scal, parts, loc)
    else:
        small = sum_small(grads[1], EX)
        grads = sum_expert(grads[0])
        proj_sum, out_weight_grad = grads[: 3 * loc], grads[3 * loc :]
    qkv_grad = jnp.swapaxes(proj_sum.reshape(3, loc, width), 1, 2)

    gains = sum_small(small[:8], TE)
    shifted = jnp.roll(column_map, -1, 0)[:, : buckets - 1]
    near_grad = jnp.dot(small[2 : 2 + heads, :TILE], shifted, precision=lax.Precision.HIGHEST)
    position_bias_grad = jnp.concatenate([near_grad, -jnp.sum(near_grad, 1, keepdims=True)], 1)

    layer_output = combine_fwd(slot_cols, gates, hidden, out_rows.reshape(-1, width))
    input_grad = finish_input(layer_input, own_part, got_near, got_far, gain_one, d_hidden)
    return (
        layer_output,
        input_grad,
        gains[0],
        qkv_grad,
        position_bias_grad,
        out_weight_grad,
        gains[1],
        up_grad,
        down_grad,
    )


def solution(mesh):
    in_specs = (
        P((EX, TE), None),
        P(EX, TE),
        P((EX, TE), None),
        P((EX, TE), None),
        P(),
        P(None, None, TE),
        P(TE, None),
        P(TE, None),
        P(),
        P(EX, None, TE),
        P(EX, TE, None),
        P((EX, TE), None),
    )
    out_specs = (
        P((EX, TE), None),
        P((EX, TE), None),
        P(),
        P(None, None, TE),
        P(TE, None),
        P(TE, None),
        P(),
        P(EX, None, TE),
        P(EX, TE, None),
    )

    return jax.shard_map(on_device, mesh=mesh, in_specs=in_specs, out_specs=out_specs, check_vma=False)
```

```python
import functools
import math

import jax
import jax.numpy as jnp
from jax import lax
from jax.experimental import pallas as pl
from jax.experimental.pallas import tpu as pltpu
from jax.sharding import PartitionSpec as P


WINDOW = 1024
TILE = 256
STRIP = 320
NEG = -1e30
EPS = 1e-06
BF = jnp.bfloat16
F32 = jnp.float32

EX, TE = "expert", "tensor"
DIAG, PREV, MASK, PLAIN = range(4)


def bucket_edges(buckets):
    half_count = buckets // 2
    edges = list(range(1, half_count))
    for power in range(half_count):
        edges.append(int(math.ceil(half_count * (128.0 / half_count) ** (power / half_count))))
    return edges


def bucket_index(distance, buckets):
    counted = jnp.zeros(distance.shape, jnp.int32)
    for edge in bucket_edges(buckets):
        counted = counted + (distance >= edge).astype(jnp.int32)
    return counted


def dot(left, right, left_dim=1, right_dim=0):
    return lax.dot_general(
        left, right, (((left_dim,), (right_dim,)), ((), ())), preferred_element_type=F32
    )


def swap(value, axis, bit):
    size = lax.axis_size(axis)
    return lax.ppermute(value, axis, [(i, i ^ bit) for i in range(size)])


def vmem(count):
    return [pl.BlockSpec(memory_space=pltpu.VMEM)] * count


def params(mib=56):
    return pltpu.CompilerParams(vmem_limit_bytes=mib << 20)


def anywhere(count):
    return [pl.BlockSpec(memory_space=pl.ANY)] * count


def shape(dims, dtype):
    return jax.ShapeDtypeStruct(dims, dtype)


def proj_kernel(scale, xa_ref, xb_ref, gain, wt_ref, *refs):
    norm, k_ref, qt, vt = refs[-4:]
    x = jnp.where(pl.program_id(0) < 2, xa_ref[...], xb_ref[...]).astype(F32)
    r = lax.rsqrt(jnp.mean(x * x, -1, keepdims=True) + EPS)
    n = (x * r * gain[...]).astype(BF)
    norm[0] = n
    k_ref[0] = dot(n, wt_ref[1], 1, 1).astype(BF)
    qt[0] = (dot(wt_ref[0], n, 1, 1) * scale).astype(BF)
    vt[0] = dot(wt_ref[2], n, 1, 1).astype(BF)


def pair_specs(width):
    return [
        pl.BlockSpec((TILE, width), lambda n: (jnp.minimum(n, 1), 0)),
        pl.BlockSpec((TILE, width), lambda n: (jnp.maximum(n - 2, 0), 0)),
    ]


def project(base, pair, gain, wt, scale, kept):
    width = pair[0].shape[1]
    loc = wt.shape[1]
    dims = ((TILE, width), (TILE, loc), (loc, TILE), (loc, TILE))
    return pl.pallas_call(
        functools.partial(proj_kernel, scale),
        grid=(4,),
        out_shape=[shape((8,) + d, BF) for d in dims],
        in_specs=pair_specs(width)
        + [
            pl.BlockSpec((1, width), lambda n: (0, 0)),
            pl.BlockSpec((3, loc, width), lambda n: (0, 0, 0)),
        ]
        + anywhere(len(kept)),
        out_specs=[pl.BlockSpec((1,) + d, lambda n: (base + n, 0, 0)) for d in dims],
        input_output_aliases={4 + n: n for n in range(len(kept))},
        compiler_params=params(),
    )(*pair, gain, wt, *kept)


def again_kernel(scale, n_ref, wt_ref, q_ref, v_ref, kt_ref):
    n = n_ref[0]
    q_ref[0] = (dot(n, wt_ref[0], 1, 1) * scale).astype(BF)
    v_ref[0] = dot(n, wt_ref[2], 1, 1).astype(BF)
    kt_ref[0] = dot(wt_ref[1], n, 1, 1).astype(BF)


def project_again(norm, wt, scale):
    tiles, _, width = norm.shape
    loc = wt.shape[1]
    nat = pl.BlockSpec((1, TILE, loc), lambda n: (n, 0, 0))
    return pl.pallas_call(
        functools.partial(again_kernel, scale),
        grid=(tiles,),
        out_shape=[shape((tiles, TILE, loc), BF)] * 2 + [shape((tiles, loc, TILE), BF)],
        in_specs=[
            pl.BlockSpec((1, TILE, width), lambda n: (n, 0, 0)),
            pl.BlockSpec((3, loc, width), lambda n: (0, 0, 0)),
        ],
        out_specs=[nat, nat, pl.BlockSpec((1, loc, TILE), lambda n: (n, 0, 0))],
        compiler_params=params(),
    )(norm, wt)


def head_rows(head, size, dims, axis):
    index = lax.broadcasted_iota(jnp.int32, dims, axis)
    return (index >= head * size) & (index < (head + 1) * size)


def first_key(q, c1, c2):
    start = jnp.where(q >= c2, c2, jnp.where(q >= c1, c1, 0))
    return jnp.maximum(start, q - (WINDOW - 1))


def build_bias(line_ref, bias_ref, heads):
    for h in range(heads):
        row = jnp.broadcast_to(line_ref[h : h + 1, :], (TILE, TILE))
        bias_ref[h] = pltpu.roll(row, 0, 1, stride=1, stride_axis=0)


def key_loop(i, c1, c2, tiles):
    start = first_key(i * TILE, c1, c2) // TILE
    full = (first_key(i * TILE + TILE - 1, c1, c2) + TILE - 1) // TILE
    carry = tiles([(i, DIAG), (i - 1, PREV)], None)
    count = jnp.maximum(i - 1 - start, 0)
    plain = jnp.minimum(jnp.maximum(i - 1 - full, 0), count)
    carry = lax.fori_loop(0, plain, lambda n, c: tiles([(i - 2 - n, PLAIN)], c), carry)
    return lax.fori_loop(plain, count, lambda n, c: tiles([(i - 2 - n, MASK)], c), carry)


def tile_masks(tiles, low, t):
    kk = lax.broadcasted_iota(jnp.int32, (TILE, TILE), 0)
    qq = lax.broadcasted_iota(jnp.int32, (TILE, TILE), 1)
    out = []
    for j, kind in tiles:
        ok = None
        if kind != PLAIN:
            ok = kk >= low - j * TILE
            if kind == DIAG:
                ok = ok & (kk <= qq)
        out.append((jnp.maximum(j, 0) ^ (2 * t), kind, ok))
    return out, qq < kk


def add_bias(s, kind, bias, wrapped):
    if kind == DIAG:
        return s + bias
    if kind == PREV:
        return s + jnp.where(wrapped, bias, 0.0)
    return s


def attn_fwd_kernel(heads, size, base, s_ref, c_ref, k_ref, qt_ref, vt_ref, line_ref, wo_ref, *refs):
    mix_ref, lse_ref, pa_ref, pb_ref, bias_ref = refs[-5:]
    t, c1, c2 = s_ref[0], c_ref[0, 0], c_ref[0, 1]
    loc = heads * size
    step = pl.program_id(0)

    @pl.when(step == 0)
    def _():
        build_bias(line_ref, bias_ref, heads)

    i = (base + step) ^ (2 * t)
    qt = qt_ref[0]
    zero = jnp.zeros_like(qt)
    qz = [jnp.where(head_rows(h, size, (loc, TILE), 0), qt, zero) for h in range(heads)]
    qpos = i * TILE + lax.broadcasted_iota(jnp.int32, (1, TILE), 1)
    low = first_key(qpos, c1, c2)

    def tiles(pairs, carry):
        pairs, wrapped = tile_masks(pairs, low, t)
        scores = []
        for h in range(heads):
            for at, kind, ok in pairs:
                s = add_bias(dot(k_ref[at], qz[h]), kind, bias_ref[h], wrapped)
                scores.append(s if ok is None else jnp.where(ok, s, NEG))
        out = []
        for h in range(heads):
            mine = scores[h * len(pairs) : (h + 1) * len(pairs)]
            m = functools.reduce(jnp.maximum, mine)
            m = jnp.max(m, 0, keepdims=True)
            if carry is not None:
                m = jnp.maximum(carry[h][0], m)
            probs = [jnp.exp(s - m) for s in mine]
            total = jnp.sum(functools.reduce(jnp.add, probs), 0, keepdims=True)
            acc = None
            for (at, _, _), p in zip(pairs, probs):
                piece = dot(vt_ref[at][h * size : (h + 1) * size], p.astype(BF))
                acc = piece if acc is None else acc + piece
            if carry is not None:
                decay = jnp.exp(carry[h][0] - m)
                total = decay * carry[h][1] + total
                acc = decay * carry[h][2] + acc
            out.append((m, total, acc))
        return tuple(out)

    final = key_loop(i, c1, c2, tiles)
    mixed = []
    for h in range(heads):
        m, total, acc = final[h]
        mixed.append((acc * (1.0 / total)).astype(BF))
        lse_ref[0, h : h + 1, :] = m + jnp.log(total)
    mixed = jnp.concatenate(mixed, 0)
    mix_ref[0] = mixed
    part = dot(mixed, wo_ref[...], 0, 0).astype(BF)

    @pl.when(step < 2)
    def _():
        pa_ref[...] = part

    @pl.when(step >= 2)
    def _():
        pb_ref[...] = part


def attn_fwd(base, scal, counts, k, qt, vt, line, wo, kept, heads, size):
    tiles, _, loc = k.shape
    width = wo.shape[1]
    tile = lambda n: (base + n, 0, 0)
    return pl.pallas_call(
        functools.partial(attn_fwd_kernel, heads, size, base),
        grid=(4,),
        out_shape=(
            shape((tiles, loc, TILE), BF),
            shape((tiles, 8, TILE), F32),
            shape((2 * TILE, width), BF),
            shape((2 * TILE, width), BF),
        ),
        in_specs=[
            pl.BlockSpec(memory_space=pltpu.SMEM),
            pl.BlockSpec(memory_space=pltpu.SMEM),
            pl.BlockSpec((tiles, TILE, loc), lambda n: (0, 0, 0)),
            pl.BlockSpec((1, loc, TILE), tile),
            pl.BlockSpec((tiles, loc, TILE), lambda n: (0, 0, 0)),
            pl.BlockSpec((8, TILE), lambda n: (0, 0)),
            pl.BlockSpec((loc, width), lambda n: (0, 0)),
        ]
        + anywhere(len(kept)),
        out_specs=(
            pl.BlockSpec((1, loc, TILE), tile),
            pl.BlockSpec((1, 8, TILE), tile),
            *pair_specs(width),
        ),
        scratch_shapes=[pltpu.VMEM((heads, TILE, TILE), F32)],
        input_output_aliases={7 + n: n for n in range(len(kept))},
        compiler_params=params(),
    )(scal, counts, k, qt, vt, line, wo, *kept)


def attn_bwd_kernel(
    heads,
    size,
    base,
    last,
    s_ref,
    c_ref,
    k_ref,
    v_ref,
    kt_ref,
    qt_ref,
    q_ref,
    da_ref,
    db_ref,
    mix_ref,
    lse_ref,
    line_ref,
    wo_ref,
    *refs,
):
    bias_ref = refs[-1]
    if last:
        dq_near, dk_in, dv_in, g_in, og_in, moe_ref, gain_ref, norm_ref, wt_ref = refs[:9]
        part_refs, outs = refs[9:13], refs[13:-10]
        dq_ref, dk_ref, dv_ref, g_ref, og_ref, sum_ref, small_ref, parts, sem = refs[-10:-1]
    else:
        dq_ref, dk_ref, dv_ref, g_ref, og_ref = refs[:-1]
    t, c1, c2 = s_ref[0], c_ref[0, 0], c_ref[0, 1]
    loc = heads * size
    step = pl.program_id(0)

    @pl.when(step == 0)
    def _():
        build_bias(line_ref, bias_ref, heads)
        if last:
            g_ref[...] = g_in[...]
            og_ref[...] = og_in[...]
            dq_ref[:, 0 : dq_near.shape[1]] = dq_near[...]
        else:
            g_ref[...] = jnp.zeros_like(g_ref)
            og_ref[...] = jnp.zeros_like(og_ref)

        def first_sums(at, _):
            dk_ref[at] = dk_in[at] if last else jnp.zeros(dk_ref.shape[1:], F32)
            dv_ref[at] = dv_in[at] if last else jnp.zeros(dv_ref.shape[1:], F32)
            return 0

        lax.fori_loop(0, dk_ref.shape[0], first_sums, 0)

    i = (base + step) ^ (2 * t)
    rows = jnp.where(step < 2, da_ref[...], db_ref[...])
    dn = dot(rows, wo_ref[...], 1, 1).astype(BF)
    dt = dot(wo_ref[...], rows, 1, 1).astype(BF)
    og_ref[...] += dot(mix_ref[0], rows)
    qt = qt_ref[0]
    qn = q_ref[0]
    zt = jnp.zeros_like(qt)
    zn = jnp.zeros_like(qn)
    rh = [head_rows(h, size, (loc, TILE), 0) for h in range(heads)]
    ch = [head_rows(h, size, (TILE, loc), 1) for h in range(heads)]
    qz = [jnp.where(rh[h], qt, zt) for h in range(heads)]
    dz = [jnp.where(rh[h], dt, zt) for h in range(heads)]
    qm = [jnp.where(ch[h], qn, zn) for h in range(heads)]
    dm = [jnp.where(ch[h], dn, zn) for h in range(heads)]
    prod = dt.astype(F32) * mix_ref[0].astype(F32)
    delta = [jnp.sum(prod[h * size : (h + 1) * size], 0, keepdims=True) for h in range(heads)]
    lse = [lse_ref[0, h : h + 1, :] for h in range(heads)]
    qpos = i * TILE + lax.broadcasted_iota(jnp.int32, (1, TILE), 1)
    low = first_key(qpos, c1, c2)

    def tiles(pairs, carry):
        pairs, wrapped = tile_masks(pairs, low, t)
        out = [None] * heads if carry is None else list(carry)
        raw = [[(dot(k_ref[at], qz[h]), dot(v_ref[at], dz[h])) for h in range(heads)] for at, _, _ in pairs]
        narrow = []
        for (at, kind, ok), products in zip(pairs, raw):
            lows = []
            for h, (s, dp) in enumerate(products):
                s = add_bias(s, kind, bias_ref[h], wrapped) - lse[h]
                if ok is not None:
                    s = jnp.where(ok, s, NEG)
                p = jnp.exp(s)
                ds = p * (dp - delta[h])
                if kind == DIAG:
                    g_ref[h] += ds
                elif kind == PREV:
                    g_ref[h] += jnp.where(wrapped, ds, 0.0)
                lows.append((p.astype(BF), ds.astype(BF)))
            narrow.append(lows)
        for (at, _, _), lows in zip(pairs, narrow):
            dv = None
            dk = None
            for h, (p, ds) in enumerate(lows):
                piece = dot(p, dm[h])
                dv = piece if dv is None else dv + piece
                piece = dot(ds, qm[h])
                dk = piece if dk is None else dk + piece
                piece = dot(kt_ref[at][h * size : (h + 1) * size], ds)
                out[h] = piece if out[h] is None else out[h] + piece
            dv_ref[at] += dv
            dk_ref[at] += dk
        return tuple(out)

    final = key_loop(i, c1, c2, tiles)
    dq = (jnp.concatenate(final, 0) * (size**-0.5)).astype(BF)
    if not last:
        dq_ref[...] = dq
        return
    dq_ref[:, pl.ds(pl.multiple_of((base + step) * TILE, TILE), TILE)] = dq

    @pl.when(step == pl.num_programs(0) - 1)
    def _():
        each = norm_ref.shape[0] // 4
        sum_ref[0 : 3 * loc] = jnp.zeros((3 * loc, sum_ref.shape[1]), F32)
        sum_ref[3 * loc : 4 * loc] = og_ref[...]

        def block(pos, _):
            span = pl.ds(pl.multiple_of(pos * each, TILE), each)
            pair = pl.ds(2 * pos, 2)
            dqt = dq_ref[:, span]
            dk = dk_ref[pair].astype(BF).reshape(each, loc)
            dv = dv_ref[pair].astype(BF).reshape(each, loc)
            n = norm_ref[span]
            sum_ref[0:loc] += dot(dqt, n)
            sum_ref[loc : 2 * loc] += dot(dk, n, 0, 0)
            sum_ref[2 * loc : 3 * loc] += dot(dv, n, 0, 0)
            part = dot(dqt, wt_ref[0], 0, 0) + dot(dk, wt_ref[1]) + dot(dv, wt_ref[2])
            parts[pos] = part.astype(BF)
            return 0

        lax.fori_loop(0, 4, block, 0)
        copies = [pltpu.make_async_copy(parts.at[pos], part_refs[pos], sem.at[pos]) for pos in range(4)]
        for copy in copies:
            copy.start()
        total = None
        for c in range(3):
            line = jnp.sum(sum_ref[c * loc : (c + 1) * loc] * wt_ref[c].astype(F32), 0, keepdims=True)
            total = line if total is None else total + line
        small_ref[...] = jnp.zeros_like(small_ref)
        small_ref[0:1] = total / gain_ref[...]
        small_ref[1:2] = moe_ref[0:1]
        kk = lax.broadcasted_iota(jnp.int32, (TILE, TILE), 0)
        qq = lax.broadcasted_iota(jnp.int32, (TILE, TILE), 1)
        flip = (kk + qq == TILE - 1).astype(F32)
        for h in range(heads):
            g = lax.dot_general(
                flip,
                g_ref[h],
                (((1,), (0,)), ((), ())),
                precision=lax.Precision.HIGHEST,
                preferred_element_type=F32,
            )
            g = pltpu.roll(g, 0, 1, stride=1, stride_axis=0)
            small_ref[2 + h : 3 + h, 0:TILE] = jnp.sum(g, 0, keepdims=True)
        if len(outs) == 2:
            outs[0][...] = sum_ref[...]
            outs[1][...] = small_ref[...]
        else:
            count = 4 * loc // len(outs)
            small = small_ref[...].astype(BF)
            for e, out in enumerate(outs):
                first = pl.multiple_of((s_ref[1] ^ e) * count, 16)
                out[0:count] = sum_ref[pl.ds(first, count)].astype(BF)
                out[count : count + 16] = small
        for copy in copies:
            copy.wait()


def attn_bwd(base, scal, counts, k, v, kt, qt, q, d_rows, mix, lse, line, wo, sums, heads, size, chunks=1):
    tiles, _, loc = k.shape
    width = wo.shape[1]
    last = bool(sums)
    tile = lambda n: (base + n, 0, 0)
    whole = lambda *dims: pl.BlockSpec(dims, lambda n: (0,) * len(dims))
    nat = whole(tiles, TILE, loc)
    square = whole(heads, TILE, TILE)
    half = tiles // 2 * TILE
    in_specs = [
        pl.BlockSpec(memory_space=pltpu.SMEM),
        pl.BlockSpec(memory_space=pltpu.SMEM),
        nat,
        nat,
        whole(tiles, loc, TILE),
        pl.BlockSpec((1, loc, TILE), tile),
        pl.BlockSpec((1, TILE, loc), tile),
        *pair_specs(width),
        pl.BlockSpec((1, loc, TILE), tile),
        pl.BlockSpec((1, 8, TILE), tile),
        whole(8, TILE),
        whole(loc, width),
    ]
    running = [(tiles, TILE, loc)] * 2 + [(heads, TILE, TILE), (loc, width)]
    if last:
        in_specs += [whole(loc, half), nat, nat, square, whole(loc, width), whole(8, width), whole(1, width)]
        in_specs += [whole(2 * half, width), whole(3, loc, width)]
        results = [((half // 2, width), BF)] * 4
        if chunks == 1:
            results += [((4 * loc, width), F32), ((16, width), F32)]
        else:
            results += [((4 * loc // chunks + 16, width), BF)] * chunks
        out_specs = anywhere(4) + [whole(*dims) for dims, _ in results[4:]]
        scratch = [pltpu.VMEM((loc, 2 * half), BF)] + [pltpu.VMEM(dims, F32) for dims in running]
        scratch += [pltpu.VMEM((4 * loc, width), F32), pltpu.VMEM((16, width), F32)]
        scratch += [pltpu.VMEM((4, half // 2, width), BF), pltpu.SemaphoreType.DMA((4,))]
    else:
        results = [((loc, half), BF)] + [(dims, F32) for dims in running]
        out_specs = [pl.BlockSpec((loc, TILE), lambda n: (0, n))] + [whole(*dims) for dims in running]
        scratch = []
    return pl.pallas_call(
        functools.partial(attn_bwd_kernel, heads, size, base, last),
        grid=(4,),
        out_shape=[shape(dims, kind) for dims, kind in results],
        in_specs=in_specs,
        out_specs=out_specs,
        scratch_shapes=scratch + [pltpu.VMEM((heads, TILE, TILE), F32)],
        compiler_params=params(),
    )(scal, counts, k, v, kt, qt, q, *d_rows, mix, lse, line, wo, *sums)


def sum_grads_kernel(*refs):
    parts, (out_ref, small_ref) = refs[:-2], refs[-2:]
    total = functools.reduce(jnp.add, [part[...].astype(F32) for part in parts])
    rows = out_ref.shape[0]
    out_ref[...] = total[0:rows].astype(BF)
    small_ref[...] = total[rows:]


def sum_grads(parts):
    rows, width = parts[0].shape
    return pl.pallas_call(
        sum_grads_kernel,
        out_shape=[shape((rows - 16, width), BF), shape((16, width), F32)],
        in_specs=vmem(len(parts)),
        out_specs=vmem(2),
        compiler_params=params(),
    )(*parts)


def unpack_kernel(s_ref, *refs):
    parts, (proj_ref, out_ref) = refs[:-2], refs[-2:]
    rows = parts[0].shape[0]
    edge = proj_ref.shape[0] // rows
    for e, part in enumerate(parts):
        at = s_ref[1] ^ e

        @pl.when(at < edge)
        def _():
            proj_ref[pl.ds(pl.multiple_of(at * rows, 16), rows)] = part[...].astype(F32)

        @pl.when(at >= edge)
        def _():
            out_ref[pl.ds(pl.multiple_of((at - edge) * rows, 16), rows)] = part[...].astype(F32)


def unpack_grads(scal, parts, loc):
    width = parts[0].shape[1]
    return pl.pallas_call(
        unpack_kernel,
        out_shape=[shape((3 * loc, width), F32), shape((loc, width), F32)],
        in_specs=[pl.BlockSpec(memory_space=pltpu.SMEM)] + vmem(len(parts)),
        out_specs=vmem(2),
        compiler_params=params(),
    )(scal, *parts)


def turn_sum_kernel(a_ref, b_ref, c_ref, out_ref):
    out_ref[...] = (a_ref[...].astype(F32) + b_ref[...].astype(F32) + c_ref[...].astype(F32)).T


def turn_sum(a, b, c):
    return pl.pallas_call(
        turn_sum_kernel,
        grid=(3,),
        out_shape=shape(a.shape[::-1], F32),
        in_specs=[pl.BlockSpec((a.shape[0], a.shape[1] // 3), lambda n: (0, n))] * 3,
        out_specs=pl.BlockSpec((a.shape[1] // 3, a.shape[0]), lambda n: (n, 0)),
        compiler_params=params(),
    )(a, b, c)


def select_rows(slot_rows, first, count, ranks):
    want = first + lax.broadcasted_iota(jnp.int32, (count, slot_rows.shape[1]), 0)
    return [(slot_rows[r : r + 1, :] == want).astype(BF) for r in ranks]


def send_grad_kernel(
    experts_all, capacity, direct, s_ref, route_ref, gate_ref, grad_ref, rows_ref, cols_ref, gcol_ref, out_ref
):
    tokens = route_ref.shape[1]
    expert = lax.broadcasted_iota(jnp.int32, (max(8, experts_all), tokens), 0)
    hit = [route_ref[r : r + 1, :] == expert for r in range(2)]
    both = hit[0].astype(BF) + hit[1].astype(BF)
    first = lax.broadcasted_iota(jnp.int32, (tokens, tokens), 0)
    later = lax.broadcasted_iota(jnp.int32, (tokens, tokens), 1)
    earlier = dot(both, (first < later).astype(BF))
    rows = []
    for mask in (0, s_ref[1] if direct else 0):
        for r in range(2):
            place = jnp.sum(jnp.where(hit[r], earlier, 0.0), 0, keepdims=True).astype(jnp.int32)
            slot = (route_ref[r : r + 1, :] ^ mask) * capacity + place
            rows.append(jnp.where(place < capacity, slot, -1))
    rows = jnp.concatenate(rows + rows, 0)
    rows_ref[...] = rows
    cols_ref[...] = rows.astype(F32).T.astype(jnp.int32)
    gates = jnp.concatenate([gate_ref[...]] * 4, 0).T
    gcol_ref[...] = gates
    grad = grad_ref[...].astype(F32)
    scaled = [(grad * gates[:, r : r + 1]).astype(BF) for r in range(2)]

    def strip(n, _):
        first = pl.multiple_of(n * STRIP, 16)
        hot = select_rows(rows_ref, first, STRIP, (0, 1))
        out_ref[pl.ds(first, STRIP)] = (dot(hot[0], scaled[0]) + dot(hot[1], scaled[1])).astype(BF)
        return 0

    lax.fori_loop(0, out_ref.shape[0] // STRIP, strip, 0)


def send_grad(scal, routes, gates, grad, experts_all, capacity, direct):
    tokens, width = grad.shape
    return pl.pallas_call(
        functools.partial(send_grad_kernel, experts_all, capacity, direct),
        out_shape=[
            shape((8, tokens), jnp.int32),
            shape((tokens, 8), jnp.int32),
            shape((tokens, 8), F32),
            shape((experts_all * capacity, width), BF),
        ],
        in_specs=[pl.BlockSpec(memory_space=pltpu.SMEM)] + vmem(3),
        out_specs=vmem(4),
        compiler_params=params(),
    )(scal, routes, gates, grad)


def send_rows_kernel(rows_each, slot_ref, x_ref, p0, r0, r2, gain, hid_ref, *refs):
    outs, joined = refs[:-1], refs[-1]
    attn = p0[...].astype(F32) + r0[...].astype(F32) + r2[...].astype(F32)
    hidden = x_ref[...].astype(F32) + attn
    hid_ref[...] = hidden
    r = lax.rsqrt(jnp.mean(hidden * hidden, -1, keepdims=True) + EPS)
    norm = (hidden * r * gain[...]).astype(BF)

    def strip(n, _):
        first = pl.multiple_of(n * STRIP, 16)
        hot = select_rows(slot_ref, first, STRIP, (2, 3))
        joined[pl.ds(first, STRIP)] = dot(hot[0] + hot[1], norm).astype(BF)
        return 0

    lax.fori_loop(0, joined.shape[0] // STRIP, strip, 0)
    for e, out in enumerate(outs):
        out[...] = joined[e * rows_each : (e + 1) * rows_each]


def send_rows(slot_rows, x, p0, r0, r2, gain, groups, rows_each):
    rows, width = x.shape
    return pl.pallas_call(
        functools.partial(send_rows_kernel, rows_each),
        out_shape=[shape((rows, width), F32)] + [shape((rows_each, width), BF)] * groups,
        in_specs=vmem(6),
        out_specs=vmem(1 + groups),
        scratch_shapes=[pltpu.VMEM((groups * rows_each, width), BF)],
        compiler_params=params(),
    )(slot_rows, x, p0, r0, r2, gain)


TOKENS = 128


def picks(slot_ref, first, base, slots):
    own = slot_ref[pl.ds(first, TOKENS), :]
    at = lax.broadcasted_iota(jnp.int32, (TOKENS, slots), 1)
    return [(own[:, base + r : base + r + 1] == at).astype(BF) for r in range(2)]


def combine_bwd_kernel(groups, slot_ref, hid_ref, gain, grad_ref, *refs):
    blocks, (dh_ref, da_ref, gg_ref, joined) = refs[:groups], refs[groups:]
    at = 0
    for block in blocks:
        joined[at : at + block.shape[0]] = block[...]
        at += block.shape[0]
    gg_ref[...] = jnp.zeros_like(gg_ref)

    def strip(n, _):
        first = pl.multiple_of(n * TOKENS, TOKENS)
        span = pl.ds(first, TOKENS)
        hot = picks(slot_ref, first, 2, joined.shape[0])
        d = dot(hot[0] + hot[1], joined[...])
        hidden = hid_ref[span]
        r = lax.rsqrt(jnp.mean(hidden * hidden, -1, keepdims=True) + EPS)
        u = hidden * r
        gg_ref[...] += jnp.sum(u * d, 0, keepdims=True)
        gd = gain[...] * d
        dv = r * (gd - u * jnp.mean(u * gd, -1, keepdims=True))
        d_hidden = grad_ref[span].astype(F32) + dv
        dh_ref[span] = d_hidden
        da_ref[span] = d_hidden.astype(BF)
        return 0

    lax.fori_loop(0, hid_ref.shape[0] // TOKENS, strip, 0)


def combine_bwd(slot_cols, hidden, gain, grad, blocks):
    rows, width = hidden.shape
    groups = len(blocks)
    return pl.pallas_call(
        functools.partial(combine_bwd_kernel, groups),
        out_shape=(shape((rows, width), F32), shape((rows, width), BF), shape((8, width), F32)),
        in_specs=vmem(4 + groups),
        out_specs=vmem(3),
        scratch_shapes=[pltpu.VMEM((groups * blocks[0].shape[0], width), BF)],
        compiler_params=params(),
    )(slot_cols, hidden, gain, grad, *blocks)


def combine_fwd_kernel(slot_ref, gate_ref, hid_ref, data_ref, out_ref):
    def strip(n, _):
        first = pl.multiple_of(n * TOKENS, TOKENS)
        span = pl.ds(first, TOKENS)
        hot = picks(slot_ref, first, 0, data_ref.shape[0])
        gates = gate_ref[span, :]
        mixture = gates[:, 0:1] * dot(hot[0], data_ref[...]) + gates[:, 1:2] * dot(hot[1], data_ref[...])
        out_ref[span] = (hid_ref[span] + mixture).astype(BF)
        return 0

    lax.fori_loop(0, hid_ref.shape[0] // TOKENS, strip, 0)


def combine_fwd(slot_cols, gates, hidden, data):
    return pl.pallas_call(
        combine_fwd_kernel,
        out_shape=shape(hidden.shape, BF),
        in_specs=vmem(4),
        out_specs=vmem(1)[0],
        compiler_params=params(),
    )(slot_cols, gates, hidden, data)


GELU_C = math.sqrt(2.0 / math.pi)
GELU_A = 0.044715


def expert_kernel(groups, rows_each, first_row, members, direct, kept, s_ref, *refs):
    refs = list(refs)
    take = lambda count: [refs.pop(0) for _ in range(count)]
    parts = 4
    ups, downs, xs = take(parts), take(parts), take(groups)
    (d_in_ref,) = take(1)
    take(4 if kept else 0)
    act_out, dpre_out, x_out, d_out = take(4)
    results = take(groups)
    up_ref, down_ref, act_ref, dpre_ref, x_all, d_all, acc_ref, in_sem, d_sem, out_sem, row_sem = refs
    rows = groups * rows_each
    span = pl.ds(first_row, rows)
    own = []
    for n, e in enumerate(members):
        source = (s_ref[1] ^ e) if direct else 0
        own.append(
            pltpu.make_async_copy(
                d_in_ref.at[source], d_all.at[pl.ds(n * rows_each, rows_each)], d_sem.at[n]
            )
        )
        own[n].start()
    for p in range(parts):
        pltpu.make_async_copy(ups[p], up_ref.at[p], in_sem.at[0, p]).start()
        pltpu.make_async_copy(downs[p], down_ref.at[p], in_sem.at[1, p]).start()
    for e in range(groups):
        x_all[e * rows_each : (e + 1) * rows_each] = xs[e][...]
    acc_ref[...] = jnp.zeros_like(acc_ref)
    for copy in own:
        copy.wait()
    joined = [
        pltpu.make_async_copy(x_all, x_out.at[span], row_sem.at[0]),
        pltpu.make_async_copy(d_all, d_out.at[span], row_sem.at[1]),
    ]
    for copy in joined:
        copy.start()

    def kept_copies(p):
        return (
            pltpu.make_async_copy(act_ref.at[p], act_out.at[p, span], out_sem.at[0, p]),
            pltpu.make_async_copy(dpre_ref.at[p], dpre_out.at[p, span], out_sem.at[1, p]),
        )

    def part(p, _):
        pltpu.make_async_copy(ups[0], up_ref.at[p], in_sem.at[0, p]).wait()
        pltpu.make_async_copy(downs[0], down_ref.at[p], in_sem.at[1, p]).wait()
        for r in range(0, rows, STRIP):
            strip = slice(r, r + STRIP)
            up = up_ref[p]
            pre = dot(x_all[strip], up)
            d_act = dot(d_all[strip], down_ref[p], 1, 1)
            sq = pre * pre
            th = jnp.tanh(pre * (GELU_C + (GELU_C * GELU_A) * sq))
            half = 0.5 + 0.5 * th
            act_ref[p, strip] = (pre * half).astype(BF)
            slope = half + (0.5 * pre) * (1.0 - th * th) * (GELU_C + (3.0 * GELU_C * GELU_A) * sq)
            d_pre = (d_act * slope).astype(BF)
            dpre_ref[p, strip] = d_pre
            acc_ref[strip] += dot(d_pre, up, 1, 1)
        for copy in kept_copies(p):
            copy.start()
        return 0

    lax.fori_loop(0, parts, part, 0)
    for e in range(groups):
        results[e][...] = acc_ref[e * rows_each : (e + 1) * rows_each].astype(BF)
    for copy in joined:
        copy.wait()
    for p in range(parts):
        for copy in kept_copies(p):
            copy.wait()


def experts(scal, ups, downs, xs, d_rows, first_row, members, direct, kept):
    width, units = ups[0].shape
    parts, groups = len(ups), len(xs)
    rows_each = xs[0].shape[0]
    rows = groups * rows_each
    total = d_rows.shape[0] * d_rows.shape[1]
    inputs = 1 + 2 * parts + groups + 1
    flat = pl.pallas_call(
        functools.partial(expert_kernel, groups, rows_each, first_row, members, direct, bool(kept)),
        out_shape=[shape((parts, total, units), BF)] * 2
        + [shape((total, width), BF)] * 2
        + [shape((rows_each, width), BF)] * groups,
        in_specs=[pl.BlockSpec(memory_space=pltpu.SMEM)]
        + anywhere(2 * parts)
        + vmem(groups)
        + anywhere(1 + len(kept)),
        out_specs=anywhere(4) + vmem(groups),
        scratch_shapes=[
            pltpu.VMEM((parts, width, units), BF),
            pltpu.VMEM((parts, units, width), BF),
            pltpu.VMEM((parts, rows, units), BF),
            pltpu.VMEM((parts, rows, units), BF),
            pltpu.VMEM((rows, width), BF),
            pltpu.VMEM((rows, width), BF),
            pltpu.VMEM((rows, width), F32),
            pltpu.SemaphoreType.DMA((2, parts)),
            pltpu.SemaphoreType.DMA((groups,)),
            pltpu.SemaphoreType.DMA((2, parts)),
            pltpu.SemaphoreType.DMA((2,)),
        ],
        input_output_aliases={inputs + n: n for n in range(len(kept))},
        compiler_params=params(58),
    )(scal, *ups, *downs, *xs, d_rows, *kept)
    return flat[:4], flat[4:]


def expert_out_kernel(order, rows_each, s_ref, act_ref, *refs):
    downs, out_ref = refs[:-1], refs[-1]
    step = pl.program_id(0)
    total = functools.reduce(jnp.add, [dot(act_ref[p], downs[p][...]) for p in range(4)]).astype(BF)
    if len(order) == 1:
        out_ref[0, pl.ds(pl.multiple_of(step * STRIP, 16), STRIP)] = total
    else:
        each = STRIP // rows_each
        for n in range(len(order) // each):

            @pl.when(step == n)
            def _():
                for m in range(each):
                    out_ref[s_ref[1] ^ order[n * each + m]] = total[m * rows_each : (m + 1) * rows_each]


def expert_out(scal, act, downs, order):
    parts, rows, units = act.shape
    width = downs[0].shape[1]
    rows_each = rows // len(order)
    return pl.pallas_call(
        functools.partial(expert_out_kernel, order, rows_each),
        grid=(rows // STRIP,),
        out_shape=shape((len(order), rows_each, width), BF),
        in_specs=[
            pl.BlockSpec(memory_space=pltpu.SMEM),
            pl.BlockSpec((parts, STRIP, units), lambda n: (0, n, 0)),
        ]
        + [pl.BlockSpec((units, width), lambda n: (0, 0))] * parts,
        out_specs=pl.BlockSpec((len(order), rows_each, width), lambda n: (0, 0, 0)),
        compiler_params=params(58),
    )(scal, act, *downs)


def expert_grad_kernel(left_ref, right_ref, *refs):
    outs, (turned, result, sem) = refs[:4], refs[4:]
    step = pl.program_id(0)

    @pl.when(step == 0)
    def _():
        turned[...] = left_ref[...].T

    def strip(n, _):
        span = pl.ds(pl.multiple_of(n * TILE, TILE), TILE)
        result[step, span] = dot(turned[span], right_ref[0]).astype(BF)
        return 0

    lax.fori_loop(0, turned.shape[0] // TILE, strip, 0)
    copies = [pltpu.make_async_copy(result.at[n], outs[3 - n], sem.at[n]) for n in range(4)]
    for n in range(4):

        @pl.when(step == n)
        def _():
            copies[n].start()

    @pl.when(step == 3)
    def _():
        for copy in copies:
            copy.wait()


def expert_grads(left, right):
    rows, width = left.shape
    units = right.shape[2]
    return pl.pallas_call(
        expert_grad_kernel,
        grid=(4,),
        out_shape=[shape((width, units), BF)] * 4,
        in_specs=[
            pl.BlockSpec((rows, width), lambda n: (0, 0)),
            pl.BlockSpec((1, rows, units), lambda n: (3 - n, 0, 0)),
        ],
        out_specs=anywhere(4),
        scratch_shapes=[
            pltpu.VMEM((width, rows), BF),
            pltpu.VMEM((4, width, units), BF),
            pltpu.SemaphoreType.DMA((4,)),
        ],
        compiler_params=params(58),
    )(left, right)


def finish_kernel(x_ref, p0, r0, r2, gain, dh_ref, out_ref):
    d = p0[...].astype(F32) + r0[...].astype(F32) + r2[...].astype(F32)
    x = x_ref[...].astype(F32)
    r = lax.rsqrt(jnp.mean(x * x, -1, keepdims=True) + EPS)
    u = x * r
    gd = gain[...] * d
    out_ref[...] = dh_ref[...] + r * (gd - u * jnp.mean(u * gd, -1, keepdims=True))


def finish_input(x, p0, r0, r2, gain, d_hidden):
    rows, width = x.shape
    strip = pl.BlockSpec((rows // 4, width), lambda n: (n, 0))
    return pl.pallas_call(
        finish_kernel,
        grid=(4,),
        out_shape=shape(x.shape, F32),
        in_specs=[strip] * 4 + [pl.BlockSpec((1, width), lambda n: (0, 0)), strip],
        out_specs=strip,
        compiler_params=params(),
    )(x, p0, r0, r2, gain, d_hidden)


def exchange(value):
    count = lax.axis_size(EX)
    parts = value.reshape(count, -1, value.shape[-1])
    return lax.all_to_all(parts, EX, 0, 0, tiled=True)


def add_low(*parts):
    return functools.reduce(jnp.add, [part.astype(F32) for part in parts]).astype(BF)


def sum_expert(value):
    me = lax.axis_index(EX)
    count = lax.axis_size(EX)
    bits = []
    bit = 1
    while bit < count:
        half = value.shape[0] // 2
        mine = (me & bit) > 0
        keep = jnp.where(mine, value[half:], value[:half])
        give = jnp.where(mine, value[:half], value[half:]).astype(BF)
        value = keep + swap(give, EX, bit).astype(F32)
        bits.append(bit)
        bit *= 2
    value = value.astype(BF)
    for bit in reversed(bits):
        mine = (me & bit) > 0
        other = swap(value, EX, bit)
        value = jnp.concatenate(
            [jnp.where(mine, other, value), jnp.where(mine, value, other)], 0
        )
    return value.astype(F32)


def sum_small(value, axis):
    bit = 1
    while bit < lax.axis_size(axis):
        value = value + swap(value, axis, bit)
        bit *= 2
    return value


def on_device(
    layer_input,
    segment_ids,
    routes,
    gate_values,
    attn_gain,
    qkv_weight,
    position_bias,
    out_weight,
    moe_gain,
    up_weight,
    down_weight,
    out_grad,
):
    rows, width = layer_input.shape
    heads, buckets = position_bias.shape
    loc = qkv_weight.shape[2]
    size = loc // heads
    lanes = lax.axis_size(EX)
    experts_all = up_weight.shape[0] * lanes
    capacity = rows * routes.shape[1] * 5 // (4 * experts_all)
    direct = lanes == 8
    groups = lanes if direct else 1
    rows_each = experts_all * capacity // groups
    t = lax.axis_index(TE)
    me = lax.axis_index(EX)
    scal = jnp.stack([t, me]).astype(jnp.int32)
    gain_one = attn_gain.reshape(1, width)
    gain_two = moe_gain.reshape(1, width)
    turned = jnp.swapaxes(qkv_weight, 1, 2)
    scale = size**-0.5

    far_x = swap(layer_input, TE, 2)
    near_x = swap(layer_input, TE, 1)
    counts = jnp.sum(
        (segment_ids.reshape(-1, 1) < jnp.arange(1, 129, dtype=jnp.int32)[None, :]).astype(jnp.int32), 0
    )
    counts = sum_small(jnp.broadcast_to(counts[None, :], (8, 128)), TE)
    last_x = swap(far_x, TE, 1)
    kept = project(0, (layer_input, near_x), gain_one, turned, scale, [])
    norm, k, qt, vt = project(4, (far_x, last_x), gain_one, turned, scale, kept)

    slot_rows, slot_cols, gates, d_send = send_grad(
        scal, routes.T, gate_values.T, out_grad, experts_all, capacity, direct
    )
    d_rows = exchange(d_send).reshape(groups, rows_each, width)

    up, down = up_weight[0], down_weight[0]
    up_near = swap(up, TE, 1)
    down_near = swap(down, TE, 1)
    up_far = swap(up, TE, 2)
    up_last = swap(up_far, TE, 1)
    down_far = swap(down, TE, 2)
    down_last = swap(down_far, TE, 1)
    ups = (up, up_near, up_far, up_last)
    downs = (down, down_near, down_far, down_last)

    last = position_bias[:, buckets - 1 :]
    column = bucket_index(jnp.arange(TILE, dtype=jnp.int32), buckets)
    column_map = (column[:, None] == jnp.arange(buckets, dtype=jnp.int32)[None, :]).astype(F32)
    line = jnp.dot(position_bias - last, column_map.T, precision=lax.Precision.HIGHEST)
    line = jnp.pad(line, ((0, 8 - heads), (0, 0)))
    common = (scal, counts, k, qt, vt, line, out_weight)
    mix, lse, far_part, give_part = attn_fwd(4, *common, [], heads, size)
    got_far = swap(add_low(far_part, swap(give_part, TE, 1)), TE, 2)
    mix, lse, own_part, give_part = attn_fwd(0, *common, [mix, lse], heads, size)
    got_near = swap(give_part, TE, 1)
    q, v, kt = project_again(norm, turned, scale)

    hidden, *sent = send_rows(
        slot_rows, layer_input, own_part, got_near, got_far, gain_two, groups, rows_each
    )
    if direct:
        xs = sent[:1] + [swap(sent[e], EX, e) for e in range(1, groups)]
        chunks = ((4, 0, 1, 2), (5, 6, 3, 7))
    else:
        xs = [exchange(sent[0]).reshape(rows_each, width)]
        chunks = ((0,),)
    order = tuple(e for chunk in chunks for e in chunk)
    kept = []
    back = [None] * groups
    first_row = 0
    for chunk in chunks:
        kept, d_in = experts(scal, ups, downs, [xs[e] for e in chunk], d_rows, first_row, chunk, direct, kept)
        first_row += len(chunk) * rows_each
        for e, block in zip(chunk, d_in):
            back[e] = swap(block, EX, e) if e else block
    if not direct:
        back = [exchange(back[0]).reshape(rows_each, width)]
    act, d_pre, x_all, d_all = kept

    up0, up1, up2, up3 = expert_grads(x_all, d_pre)
    down0, down1, down2, down3 = expert_grads(d_all, act)
    out_rows = exchange(expert_out(scal, act, downs, order))

    def gather_grad(near, far, cross):
        near = swap(near, TE, 1)
        cross = swap(cross, TE, 1)
        return near, swap(add_low(far, cross), TE, 2)

    near, far = gather_grad(up1, up2, up3)
    up_grad = (up0.astype(F32) + near.astype(F32) + far.astype(F32))[None]
    near, far = gather_grad(down1, down2, down3)
    down_grad = turn_sum(down0, near, far)[None]

    d_hidden, d_attn, moe_part = combine_bwd(slot_cols, hidden, gain_two, out_grad, back)
    far_d = swap(d_attn, TE, 2)
    near_d = swap(d_attn, TE, 1)
    last_d = swap(far_d, TE, 1)
    common = (scal, counts, k, v, kt, qt, q)
    rest = (mix, lse, line, out_weight)
    sums = attn_bwd(0, *common, (d_attn, near_d), *rest, [], heads, size)
    flat_norm = norm.reshape(4 * rows, width)
    own_part, give_part, far_part, give_far, *grads = attn_bwd(
        4, *common, (far_d, last_d), *rest, [*sums, moe_part, gain_one, flat_norm, turned], heads, size,
        groups if direct else 1,
    )
    got_far = swap(add_low(far_part, swap(give_far, TE, 1)), TE, 2)
    got_near = swap(give_part, TE, 1)
    if direct:
        pairs = [add_low(grads[2 * j], swap(grads[2 * j + 1], EX, 1)) for j in range(4)]
        mine, small = sum_grads([pairs[0]] + [swap(pairs[j], EX, 2 * j) for j in range(1, 4)])
        column_of = [mine] + [swap(mine, EX, 2 * j) for j in range(1, 4)]
        parts = []
        for part in column_of:
            parts += [part, swap(part, EX, 1)]
        proj_sum, out_weight_grad = unpack_grads(scal, parts, loc)
    else:
        small = sum_small(grads[1], EX)
        grads = sum_expert(grads[0])
        proj_sum, out_weight_grad = grads[: 3 * loc], grads[3 * loc :]
    qkv_grad = jnp.swapaxes(proj_sum.reshape(3, loc, width), 1, 2)

    gains = sum_small(small[:8], TE)
    shifted = jnp.roll(column_map, -1, 0)[:, : buckets - 1]
    near_grad = jnp.dot(small[2 : 2 + heads, :TILE], shifted, precision=lax.Precision.HIGHEST)
    position_bias_grad = jnp.concatenate([near_grad, -jnp.sum(near_grad, 1, keepdims=True)], 1)

    layer_output = combine_fwd(slot_cols, gates, hidden, out_rows.reshape(-1, width))
    input_grad = finish_input(layer_input, own_part, got_near, got_far, gain_one, d_hidden)
    return (
        layer_output,
        input_grad,
        gains[0],
        qkv_grad,
        position_bias_grad,
        out_weight_grad,
        gains[1],
        up_grad,
        down_grad,
    )


def solution(mesh):
    in_specs = (
        P((EX, TE), None),
        P(EX, TE),
        P((EX, TE), None),
        P((EX, TE), None),
        P(),
        P(None, None, TE),
        P(TE, None),
        P(TE, None),
        P(),
        P(EX, None, TE),
        P(EX, TE, None),
        P((EX, TE), None),
    )
    out_specs = (
        P((EX, TE), None),
        P((EX, TE), None),
        P(),
        P(None, None, TE),
        P(TE, None),
        P(TE, None),
        P(),
        P(EX, None, TE),
        P(EX, TE, None),
    )

    return jax.shard_map(on_device, mesh=mesh, in_specs=in_specs, out_specs=out_specs, check_vma=False)
```
